512 devices in a mesh: ctx: 32 (over z, x), ch: 16 (over y, core).
Axes of the slice: x: 4, y: 8, z: 8, core: 2. Of those that a mesh axis runs over, the one named last changes fastest.
Arguments:
- query_seq: bfloat16 [4096, 4096], P('ctx', 'ch'), may hold values from -6 to 6
- key_seq: bfloat16 [4096, 4096], P('ctx', 'ch'), may hold values from -6 to 6
- value_seq: bfloat16 [4096, 4096], P('ctx', 'ch'), may hold values from -6 to 6
- out_grad: bfloat16 [4096, 4096], P('ctx', 'ch'), may hold values from -6 to 6
- filters: bfloat16 [4096, 256], P('ctx', 'ch'), may hold values from -6 to 6
- skip_gain: float32 [4096], P('ch'), may hold values from -1 to 1
- reaches: int32 [256], P('ch'), may hold values from 1 to 32, as said below
Outputs:
- mixed: bfloat16 [4096, 4096], P('ctx', 'ch')
- query_grad: bfloat16 [4096, 4096], P('ctx', 'ch')
- key_grad: bfloat16 [4096, 4096], P('ctx', 'ch')
- value_grad: bfloat16 [4096, 4096], P('ctx', 'ch')
- filter_grad: float32 [4096, 256], P('ctx', 'ch')
- skip_grad: float32 [4096], P('ch')
The draws below stay inside these ranges and needn't reach their ends.
Inputs may be any that keep to these rules, and one draw needn't show every extreme that they name: Each group's reach counts its own span; some group reaches the whole context and some group only its own span.
All inputs are finite; a program needn't handle non-finite values.
Results may differ from the reference program's by a relative error of at most 0.01.
Values may be sent and summed in bfloat16 or wider, within the bound.
No kernel may reach another device: no remote copies, remote signals or barrier semaphores. Data moves between devices by JAX's collectives and lax.ppermute only.
A program may use at most 64 MiB of HBM per device.

```python
import math
import jax
import jax.numpy as jnp
from jax import lax

D = 4096
GROUP = 16
TOK_DEV = 128
SPANS = 32
SEQ = 4096
G = 256


def draw_reaches(key, part):
    first, second, third = jax.random.split(key, 3)
    values = jax.random.randint(first, (G,), 1, SPANS + 1)
    longest = jax.random.randint(second, (), 0, G)
    shortest = (longest + 1 + jax.random.randint(third, (), 0, G - 1)) % G
    values = values.at[longest].set(SPANS)
    values = values.at[shortest].set(1)
    return values.astype(jnp.int32)


def level_of(rng, shape, shards, least, high):
    factor_of = 1.0
    for axis_at, shards_of in shards:
        heights = jax.random.uniform(jax.random.fold_in(jax.random.fold_in(rng, 6), axis_at), (shards_of,), jnp.float32, least / len(shards), high / len(shards))
        factor_of = factor_of * jnp.repeat(jnp.exp(heights), shape[axis_at] // shards_of).reshape((-1,) + (1,) * (len(shape) - 1 - axis_at))
    return factor_of


def normal_values(own_key, shape, scale, bound, cuts=(), kind=jnp.bfloat16):
    values = jax.random.normal(own_key, shape, jnp.float32) * scale
    if len(cuts) > 0:
        values = level_of(own_key, shape, cuts, -0.22, 0.18) * values
    return jnp.clip(values, min=-bound, max=bound).astype(kind)


def setup_inputs(seed: int = 0) -> dict:
    keys = jax.random.split(jax.random.key(seed), 8)
    query_seq = normal_values(keys[0], (SEQ, D), 1.0, 6.0, ((0, 32), (1, 16)))
    key_seq = normal_values(keys[1], (SEQ, D), 1.0, 6.0, ((0, 32), (1, 16)))
    value_seq = normal_values(keys[2], (SEQ, D), 1.0, 6.0, ((0, 32), (1, 16)))
    out_grad = normal_values(keys[3], (SEQ, D), 1.0, 6.0, ((0, 32), (1, 16)))
    filters = normal_values(keys[4], (SEQ, G), 1.0, 6.0, ((0, 32), (1, 16)))
    skip_gain = jnp.clip(jax.random.uniform(keys[5], (D,), jnp.float32, -1.0, 1.0) * level_of(keys[5], (D,), ((0, 16),), -0.4, 0.0), -1.0, 1.0)
    reaches = draw_reaches(jax.random.fold_in(keys[7], 71), 0)
    return dict(query_seq=query_seq, key_seq=key_seq, value_seq=value_seq, out_grad=out_grad, filters=filters, skip_gain=skip_gain, reaches=reaches)


def toeplitz(window):
    size_two, groups = window.shape
    block_len = size_two // 2
    flipped = window[::-1].T
    tiled = jnp.tile(flipped, (1, block_len))
    shaped = tiled[:, :block_len * (2 * block_len - 1)].reshape(groups, block_len, 2 * block_len - 1)
    return shaped[:, :, block_len - 1:]

def diag_sum(prods):
    groups, block_len, _ = prods.shape
    padded = jnp.pad(prods, ((0, 0), (0, 0), (block_len - 1, 0)))
    flat = padded.reshape(groups, block_len * (2 * block_len - 1))
    flat = jnp.pad(flat, ((0, 0), (0, block_len)))
    sums = flat.reshape(groups, block_len, 2 * block_len).sum(axis=1)
    return sums[:, ::-1].T

def reference(query_seq, key_seq, value_seq, out_grad, filters, skip_gain, reaches):
    f32 = jnp.float32
    block_len = TOK_DEV
    scale = 1.0 / math.sqrt(SEQ)
    groups = D // GROUP
    z_vals = (key_seq.astype(f32) * value_seq.astype(f32)).astype(jnp.bfloat16)
    grads = (out_grad.astype(f32) * query_seq.astype(f32)).astype(jnp.bfloat16)
    z_blocks = z_vals.astype(f32).reshape(SPANS, block_len, groups, GROUP)
    g_blocks = grads.astype(f32).reshape(SPANS, block_len, groups, GROUP)
    z_padded = jnp.concatenate([jnp.zeros_like(z_blocks), z_blocks], axis=0)
    g_padded = jnp.concatenate([g_blocks, jnp.zeros_like(g_blocks)], axis=0)
    taps = jnp.concatenate([jnp.zeros((block_len, groups), jnp.bfloat16), filters], axis=0)
    high = lax.Precision.HIGHEST

    def step(offset, carry):
        filtered, back_sum, tap_sums = carry
        offset = jnp.asarray(offset).astype(jnp.int32)
        window = lax.dynamic_slice_in_dim(taps, offset * block_len, 2 * block_len, 0)
        weights = (offset < reaches).astype(f32)
        tmat = toeplitz(window).astype(f32) * weights[:, None, None]
        shifted = lax.dynamic_slice_in_dim(z_padded, (SPANS - offset).astype(jnp.int32), SPANS, 0)
        later = lax.dynamic_slice_in_dim(g_padded, offset, SPANS, 0)
        filtered = filtered + jnp.einsum('gab,nbgc->nagc', tmat, shifted, precision=high)
        back_sum = back_sum + jnp.einsum('gab,nagc->nbgc', tmat, later, precision=high)
        prods = jnp.einsum('nagc,nbgc->gab', g_blocks, shifted, precision=high) * weights[:, None, None]
        current = lax.dynamic_slice_in_dim(tap_sums, offset * block_len, 2 * block_len, 0)
        tap_sums = lax.dynamic_update_slice_in_dim(tap_sums, current + diag_sum(prods), offset * block_len, 0)
        return (filtered, back_sum, tap_sums)
    start = (jnp.zeros_like(z_blocks), jnp.zeros_like(z_blocks), jnp.zeros((SEQ + block_len, groups), f32))
    filtered, back_sum, tap_sums = lax.fori_loop(0, SPANS, step, start)
    filtered = filtered.reshape(SEQ, D) * scale
    back_sum = back_sum.reshape(SEQ, D) * scale
    total = filtered + skip_gain[None, :] * z_vals.astype(f32)
    mixed = (query_seq.astype(f32) * total).astype(jnp.bfloat16)
    query_grad = (out_grad.astype(f32) * total).astype(jnp.bfloat16)
    back_total = back_sum + skip_gain[None, :] * grads.astype(f32)
    key_grad = (back_total * value_seq.astype(f32)).astype(jnp.bfloat16)
    value_grad = (back_total * key_seq.astype(f32)).astype(jnp.bfloat16)
    filter_grad = tap_sums[block_len:] * scale
    skip_grad = lax.optimization_barrier(jnp.sum(grads.astype(f32) * z_vals.astype(f32), axis=0))
    return (mixed, query_grad, key_grad, value_grad, filter_grad, skip_grad)
```

```python
import math

import jax
import jax.numpy as jnp
from jax import lax
from jax.experimental import pallas as pl
from jax.experimental.pallas import tpu as pltpu
from jax.sharding import PartitionSpec as P

GROUP = 16
ROWS = 24
F32 = jnp.float32
BF16 = jnp.bfloat16


def eye(size, flip):
    row = lax.broadcasted_iota(jnp.int32, (size, size), 0)
    col = lax.broadcasted_iota(jnp.int32, (size, size), 1)
    hit = (row + col == size - 1) if flip else (row == col)
    return jnp.where(hit, 1.0, 0.0).astype(BF16)


def matmul(lhs, rhs):
    return jnp.dot(lhs, rhs, preferred_element_type=F32)


def matmul_nt(lhs, rhs):
    return lax.dot_general(lhs, rhs, (((1,), (1,)), ((), ())), preferred_element_type=F32)


def product(first, second):
    return (first.astype(F32) * second.astype(F32)).astype(BF16)


def pack_body(query, key, value, cotangent, taps, packed):
    spans = packed.shape[0]
    block_len = query.shape[0]
    z_rows = product(key[...], value[...]).astype(F32).T
    g_rows = product(cotangent[...], query[...]).astype(F32).T
    tap_rows = taps[...].astype(F32)
    for dest in range(spans):
        group = dest * 8 // GROUP
        tail = jnp.broadcast_to(tap_rows[group : group + 1], (8, block_len))
        tile = jnp.concatenate(
            [z_rows[dest * 8 : dest * 8 + 8], g_rows[dest * 8 : dest * 8 + 8], tail], axis=0
        )
        packed[dest] = tile.astype(BF16)


def conv_body(reaches, packed, out, toep, shifted):
    spans, _, block_len = packed.shape
    wide = 2 * block_len
    half = spans // 2
    reach = reaches[lax.axis_index("ctx") * 8 // GROUP]
    row = lax.broadcasted_iota(jnp.int32, (block_len, block_len), 0)
    col = lax.broadcasted_iota(jnp.int32, (block_len, block_len), 1)
    upper = col >= row
    flip = eye(block_len, True)

    tiles = [packed[span].astype(F32) for span in range(spans)]
    z_list = [tile[0:8] for tile in tiles]
    g_list = [tile[8:16] for tile in tiles]
    weights = [(offset < reach).astype(F32) for offset in range(spans)]

    toep[:, 0:block_len] = jnp.zeros((block_len, block_len), BF16)
    before = jnp.zeros((block_len, block_len), F32)
    for offset in range(spans):
        window = jnp.broadcast_to(tiles[offset][16:17], (block_len, block_len))
        turned = pltpu.roll(window, 0, 1, stride=1, stride_axis=0)
        block = jnp.where(upper, turned, before) * weights[offset]
        toep[:, (offset + 1) * block_len : (offset + 2) * block_len] = block.astype(BF16)
        before = turned

    g_all = jnp.concatenate(g_list, axis=0).astype(BF16)
    g_flip = matmul(g_all, flip)

    parts = []
    for pair in range(half):
        first = 2 * pair
        parts.append(jnp.concatenate([z_list[first], z_list[first + 1]], axis=1))
        low, high = (spans - 1 - first) * 8, (spans - 2 - first) * 8
        parts.append(jnp.concatenate([g_flip[low : low + 8], g_flip[high : high + 8]], axis=1))
    data = jnp.concatenate(parts, axis=0).astype(BF16)
    acc = None
    for offset in range(half):
        base = 2 * offset * block_len
        block = jnp.concatenate(
            [toep[:, base + block_len : base + block_len + wide], toep[:, base : base + wide]], axis=0
        )
        term = matmul(data[: (half - offset) * 16], block)
        if acc is None:
            acc = term
        else:
            acc = jnp.concatenate([acc[: offset * 16], acc[offset * 16 :] + term], axis=0)

    z_flip = matmul(jnp.concatenate(z_list, axis=0).astype(BF16), flip)
    z_down = jnp.concatenate([jnp.zeros((8, block_len), F32), z_flip[:-8]], axis=0)
    shifted[0 : spans * 8] = jnp.zeros((spans * 8, wide), BF16)
    shifted[spans * 8 : spans * 16] = jnp.concatenate([z_flip, z_down], axis=1).astype(BF16)
    g_turn = jnp.concatenate(g_list, axis=0).T.astype(BF16)
    turned = []
    for pair in range(half):
        start = spans * 8 - 16 * pair
        prods = matmul(g_turn, shifted[start : start + spans * 8])
        for side in range(2):
            own = prods[:, side * block_len : (side + 1) * block_len] * weights[2 * pair + side]
            turned.append(pltpu.roll(own, 1, 1, stride=1, stride_axis=0))
    turned.append(jnp.zeros((block_len, block_len), F32))

    skip = jnp.zeros((8, block_len), F32)
    for span in range(spans):
        skip = skip + z_list[span] * g_list[span]
    skip = jnp.sum(skip, axis=1, keepdims=True)
    lane = lax.broadcasted_iota(jnp.int32, (8, block_len), 1)
    sub = lax.broadcasted_iota(jnp.int32, (8, block_len), 0)
    skip_row = jnp.sum(jnp.where(lane % 8 == sub, skip, 0.0), axis=0, keepdims=True)
    skip_high = skip_row.astype(BF16).astype(F32)
    skip_low = skip_row - skip_high

    for span in range(spans):
        pair, side = span // 2, span % 2
        forth = acc[pair * 16 : pair * 16 + 8, side * block_len : (side + 1) * block_len]
        mirror = spans - 1 - span
        pair, side = mirror // 2, mirror % 2
        back = acc[pair * 16 + 8 : pair * 16 + 16, side * block_len : (side + 1) * block_len]
        sums = jnp.sum(jnp.where(col <= row, turned[span], turned[span + 1]), axis=0, keepdims=True)
        high = sums.astype(BF16).astype(F32)
        low = sums - high
        tail = jnp.where(
            sub == 0, high, jnp.where(sub == 1, low, jnp.where(sub == 2, skip_high, skip_low))
        )
        out[span] = jnp.concatenate([forth, back, tail], axis=0).astype(BF16)


def gate_body(scale, query, key, value, cotangent, gain, packed, mixed, query_grad, key_grad, value_grad, tap_grad, skip_grad):
    spans, _, block_len = packed.shape
    tiles = [packed[span].astype(F32) for span in range(spans)]
    forth = jnp.concatenate([tile[0:8] for tile in tiles], axis=0).astype(BF16)
    back = jnp.concatenate([tile[8:16] for tile in tiles], axis=0).astype(BF16)
    flip = eye(block_len, True)
    filtered = matmul_nt(eye(block_len, False), forth) * scale
    back_sum = matmul_nt(flip, back) * scale
    q_val, k_val = query[...].astype(F32), key[...].astype(F32)
    v_val, o_val = value[...].astype(F32), cotangent[...].astype(F32)
    z_val = (k_val * v_val).astype(BF16).astype(F32)
    g_val = (o_val * q_val).astype(BF16).astype(F32)
    total = filtered + gain[...] * z_val
    mixed[...] = (q_val * total).astype(BF16)
    query_grad[...] = (o_val * total).astype(BF16)
    back_total = back_sum + gain[...] * g_val
    key_grad[...] = (back_total * v_val).astype(BF16)
    value_grad[...] = (back_total * k_val).astype(BF16)

    per_group = GROUP // 8
    for group in range(spans // per_group):
        rows = tiles[group * per_group][16:24]
        both = [rows[0:1], rows[1:2]]
        for member in range(1, per_group):
            rows = tiles[group * per_group + member][16:24]
            both = [both[0] + rows[0:1], both[1] + rows[1:2]]
        tap_grad[group : group + 1] = (both[0] + both[1]) * scale

    lane = lax.broadcasted_iota(jnp.int32, (1, block_len), 1)
    for part in range(skip_grad.shape[1] // block_len):
        line = jnp.zeros((1, block_len), F32)
        for place in range(block_len // 8):
            rows = tiles[part * (block_len // 8) + place][16:24]
            line = jnp.where(lane // 8 == place, rows[2:3] + rows[3:4], line)
        skip_grad[:, part * block_len : (part + 1) * block_len] = line


def whole(space=pltpu.VMEM):
    return pl.BlockSpec(memory_space=space)


def body(query_seq, key_seq, value_seq, out_grad, filters, skip_gain, reaches):
    block_len, local_width = query_seq.shape
    spans = lax.axis_size("ctx")
    local_groups = local_width // GROUP
    scale = 1.0 / math.sqrt(block_len * spans)
    packed_shape = jax.ShapeDtypeStruct((spans, ROWS, block_len), BF16)
    params = pltpu.CompilerParams(vmem_limit_bytes=48 * 1024 * 1024)

    packed = pl.pallas_call(
        pack_body,
        out_shape=packed_shape,
        in_specs=[whole()] * 5,
        out_specs=whole(),
        compiler_params=params,
        name="pack",
    )(query_seq, key_seq, value_seq, out_grad, filters.T)
    packed = lax.all_to_all(packed, "ctx", 0, 0, tiled=True)
    packed = pl.pallas_call(
        conv_body,
        out_shape=packed_shape,
        in_specs=[whole(space=pltpu.SMEM), whole()],
        out_specs=whole(),
        scratch_shapes=[
            pltpu.VMEM((block_len, (spans + 1) * block_len), BF16),
            pltpu.VMEM((spans * 16, 2 * block_len), BF16),
        ],
        compiler_params=params,
        name="conv",
    )(reaches, packed)
    packed = lax.all_to_all(packed, "ctx", 0, 0, tiled=True)
    act = jax.ShapeDtypeStruct((block_len, local_width), BF16)
    mixed, query_grad, key_grad, value_grad, tap_grad, skip_grad = pl.pallas_call(
        lambda *refs: gate_body(scale, *refs),
        out_shape=(
            act,
            act,
            act,
            act,
            jax.ShapeDtypeStruct((local_groups, block_len), F32),
            jax.ShapeDtypeStruct((1, local_width), F32),
        ),
        in_specs=[whole()] * 6,
        out_specs=[whole()] * 6,
        compiler_params=params,
        name="gate",
    )(query_seq, key_seq, value_seq, out_grad, skip_gain[None, :], packed)
    return (mixed, query_grad, key_grad, value_grad, tap_grad.T, skip_grad[0])


def solution(mesh):
    spec = P("ctx", "ch")
    return jax.shard_map(
        body,
        mesh=mesh,
        in_specs=(spec, spec, spec, spec, spec, P("ch"), P("ch")),
        out_specs=(spec, spec, spec, spec, spec, P("ch")),
        check_vma=False,
    )
```

```python
import functools
import math

import jax
import jax.numpy as jnp
from jax import lax
from jax.experimental import pallas as pl
from jax.experimental.pallas import tpu as pltpu
from jax.sharding import PartitionSpec as P

GROUP = 16
ROWS = 24
F32 = jnp.float32
BF16 = jnp.bfloat16


def eye(size, flip):
    row = lax.broadcasted_iota(jnp.int32, (size, size), 0)
    col = lax.broadcasted_iota(jnp.int32, (size, size), 1)
    hit = (row + col == size - 1) if flip else (row == col)
    return jnp.where(hit, 1.0, 0.0).astype(BF16)


def matmul(lhs, rhs):
    return jnp.dot(lhs, rhs, preferred_element_type=F32)


def matmul_nt(lhs, rhs):
    return lax.dot_general(lhs, rhs, (((1,), (1,)), ((), ())), preferred_element_type=F32)


def product(first, second):
    return (first.astype(F32) * second.astype(F32)).astype(BF16)


def pack_body(query, key, value, cotangent, taps, gain, reaches, packed, gain_out, reach_out, q_buf, k_buf, v_buf, o_buf, t_buf, sems):
    spans, _, block_len = packed.shape
    moves = [
        pltpu.make_async_copy(source, target, sems.at[place])
        for place, (source, target) in enumerate(
            [
                (key, k_buf),
                (value, v_buf),
                (cotangent, o_buf),
                (query, q_buf),
                (taps, t_buf),
                (gain, gain_out),
                (reaches, reach_out),
            ]
        )
    ]
    for move in moves:
        move.start()
    moves[0].wait()
    moves[1].wait()
    z_rows = product(k_buf[...], v_buf[...]).astype(F32).T
    moves[2].wait()
    moves[3].wait()
    g_rows = product(o_buf[...], q_buf[...]).astype(F32).T
    moves[4].wait()
    tap_rows = t_buf[...].astype(F32)
    for dest in range(spans):
        group = dest * 8 // GROUP
        tail = jnp.broadcast_to(tap_rows[group : group + 1], (8, block_len))
        tile = jnp.concatenate(
            [z_rows[dest * 8 : dest * 8 + 8], g_rows[dest * 8 : dest * 8 + 8], tail], axis=0
        )
        packed[dest] = tile.astype(BF16)
    moves[5].wait()
    moves[6].wait()


def conv_body(scale, reaches, gain, packed, out, toep, shifted):
    spans, _, block_len = packed.shape
    wide = 2 * block_len
    half = spans // 2
    owner = lax.axis_index("ctx")
    place = lax.broadcasted_iota(jnp.int32, (1, reaches.shape[1]), 1)
    reach = jnp.sum(jnp.where(place == owner * 8 // GROUP, reaches[...].astype(F32), 0.0), axis=1, keepdims=True)
    place = lax.broadcasted_iota(jnp.int32, (8, gain.shape[1]), 1)
    channel = lax.broadcasted_iota(jnp.int32, (8, gain.shape[1]), 0) + owner * 8
    own_gain = jnp.sum(jnp.where(place == channel, gain[...], 0.0), axis=1, keepdims=True)
    row = lax.broadcasted_iota(jnp.int32, (block_len, block_len), 0)
    col = lax.broadcasted_iota(jnp.int32, (block_len, block_len), 1)
    upper = col >= row
    flip = eye(block_len, True)

    tiles = [packed[span].astype(F32) for span in range(spans)]
    z_list = [tile[0:8] for tile in tiles]
    g_list = [tile[8:16] for tile in tiles]
    reach = jnp.broadcast_to(reach, (8, block_len))
    weights = [
        jnp.concatenate([jnp.where(reach > offset, 1.0, 0.0)] * (block_len // 8), axis=0)
        for offset in range(spans)
    ]

    toep[:, 0:block_len] = jnp.zeros((block_len, block_len), BF16)
    before = jnp.zeros((block_len, block_len), F32)
    for offset in range(spans):
        window = jnp.broadcast_to(tiles[offset][16:17], (block_len, block_len))
        turned = pltpu.roll(window, 0, 1, stride=1, stride_axis=0)
        block = jnp.where(upper, turned, before) * weights[offset]
        toep[:, (offset + 1) * block_len : (offset + 2) * block_len] = block.astype(BF16)
        before = turned

    g_all = jnp.concatenate(g_list, axis=0).astype(BF16)
    g_flip = matmul(g_all, flip)

    parts = []
    for pair in range(half):
        first = 2 * pair
        parts.append(jnp.concatenate([z_list[first], z_list[first + 1]], axis=1))
        low, high = (spans - 1 - first) * 8, (spans - 2 - first) * 8
        parts.append(jnp.concatenate([g_flip[low : low + 8], g_flip[high : high + 8]], axis=1))
    data = jnp.concatenate(parts, axis=0).astype(BF16)
    acc = None
    for offset in range(half):
        base = 2 * offset * block_len
        block = jnp.concatenate(
            [toep[:, base + block_len : base + block_len + wide], toep[:, base : base + wide]], axis=0
        )
        term = matmul(data[: (half - offset) * 16], block)
        if acc is None:
            acc = term
        else:
            acc = jnp.concatenate([acc[: offset * 16], acc[offset * 16 :] + term], axis=0)

    z_flip = matmul(jnp.concatenate(z_list, axis=0).astype(BF16), flip)
    z_down = jnp.concatenate([jnp.zeros((8, block_len), F32), z_flip[:-8]], axis=0)
    shifted[0 : spans * 8] = jnp.zeros((spans * 8, wide), BF16)
    shifted[spans * 8 : spans * 16] = jnp.concatenate([z_flip, z_down], axis=1).astype(BF16)
    g_turn = jnp.concatenate(g_list, axis=0).T.astype(BF16)
    turned = []
    for pair in range(half):
        start = spans * 8 - 16 * pair
        prods = matmul(g_turn, shifted[start : start + spans * 8])
        for side in range(2):
            own = prods[:, side * block_len : (side + 1) * block_len] * weights[2 * pair + side]
            turned.append(pltpu.roll(own, 1, 1, stride=1, stride_axis=0))
    turned.append(jnp.zeros((block_len, block_len), F32))

    skip = jnp.zeros((8, block_len), F32)
    for span in range(spans):
        skip = skip + z_list[span] * g_list[span]
    skip = jnp.sum(skip, axis=1, keepdims=True)
    lane = lax.broadcasted_iota(jnp.int32, (8, block_len), 1)
    sub = lax.broadcasted_iota(jnp.int32, (8, block_len), 0)
    skip_row = jnp.sum(jnp.where(lane % 8 == sub, skip, 0.0), axis=0, keepdims=True)
    skip_high = skip_row.astype(BF16).astype(F32)
    skip_low = skip_row - skip_high

    for span in range(spans):
        pair, side = span // 2, span % 2
        forth = acc[pair * 16 : pair * 16 + 8, side * block_len : (side + 1) * block_len]
        mirror = spans - 1 - span
        pair, side = mirror // 2, mirror % 2
        back = acc[pair * 16 + 8 : pair * 16 + 16, side * block_len : (side + 1) * block_len]
        sums = jnp.sum(jnp.where(col <= row, turned[span], turned[span + 1]), axis=0, keepdims=True)
        high = sums.astype(BF16).astype(F32)
        low = sums - high
        tail = jnp.where(
            sub == 0, high, jnp.where(sub == 1, low, jnp.where(sub == 2, skip_high, skip_low))
        )
        forth = forth * scale + own_gain * z_list[span]
        back = back * scale + own_gain * g_flip[span * 8 : span * 8 + 8]
        out[span] = jnp.concatenate([forth, back, tail], axis=0).astype(BF16)


def gate_body(scale, query, key, value, cotangent, packed, mixed, query_grad, key_grad, value_grad, tap_grad, skip_grad, q_buf, o_buf, k_buf, v_buf, t_buf, s_buf, sems):
    spans, _, block_len = packed.shape
    moves = []

    def send(source, target):
        moves.append(pltpu.make_async_copy(source, target, sems.at[len(moves)]))
        moves[-1].start()

    tiles = [packed[span].astype(F32) for span in range(spans)]
    forth = jnp.concatenate([tile[0:8] for tile in tiles], axis=0).astype(BF16)
    total = matmul_nt(eye(block_len, False), forth)
    q_buf[...] = (query[...].astype(F32) * total).astype(BF16)
    send(q_buf, mixed)
    o_buf[...] = (cotangent[...].astype(F32) * total).astype(BF16)
    send(o_buf, query_grad)
    back = jnp.concatenate([tile[8:16] for tile in tiles], axis=0).astype(BF16)
    total = matmul_nt(eye(block_len, True), back)
    k_buf[...] = (value[...].astype(F32) * total).astype(BF16)
    send(k_buf, key_grad)
    v_buf[...] = (key[...].astype(F32) * total).astype(BF16)
    send(v_buf, value_grad)

    per_group = GROUP // 8
    for group in range(spans // per_group):
        line = jnp.zeros((1, block_len), F32)
        for member in range(per_group):
            rows = tiles[group * per_group + member][16:24]
            line = line + (rows[0:1] + rows[1:2])
        t_buf[group : group + 1] = line * scale
    send(t_buf, tap_grad)

    lane = lax.broadcasted_iota(jnp.int32, (1, block_len), 1)
    for part in range(s_buf.shape[1] // block_len):
        line = jnp.zeros((1, block_len), F32)
        for place in range(block_len // 8):
            rows = tiles[part * (block_len // 8) + place][16:24]
            line = jnp.where(lane // 8 == place, rows[2:3] + rows[3:4], line)
        s_buf[:, part * block_len : (part + 1) * block_len] = line
    send(s_buf, skip_grad)
    for move in moves:
        move.wait()


def whole(space=pltpu.VMEM):
    return pl.BlockSpec(memory_space=space)


def body(query_seq, key_seq, value_seq, out_grad, filters, skip_gain, reaches):
    block_len, local_width = query_seq.shape
    spans = lax.axis_size("ctx")
    local_groups = local_width // GROUP
    scale = 1.0 / math.sqrt(block_len * spans)
    packed_shape = jax.ShapeDtypeStruct((spans, ROWS, block_len), BF16)
    params = pltpu.CompilerParams(vmem_limit_bytes=48 * 1024 * 1024)

    act = jax.ShapeDtypeStruct((block_len, local_width), BF16)
    act_buf = pltpu.VMEM((block_len, local_width), BF16)

    sources = [query_seq, key_seq, value_seq, out_grad, filters.T, skip_gain[None, :], reaches[None, :]]
    packed, gain, reaches = pl.pallas_call(
        pack_body,
        out_shape=(
            packed_shape,
            jax.ShapeDtypeStruct((1, local_width), F32),
            jax.ShapeDtypeStruct((1, local_groups), jnp.int32),
        ),
        in_specs=[whole(pltpu.HBM)] * 7,
        out_specs=[whole()] * 3,
        scratch_shapes=[act_buf] * 4
        + [pltpu.VMEM((local_groups, block_len), BF16), pltpu.SemaphoreType.DMA((7,))],
        compiler_params=params,
        name="pack",
    )(*[pltpu.with_memory_space_constraint(x, pltpu.HBM) for x in sources])
    packed = lax.all_to_all(packed, "ctx", 0, 0, tiled=True)
    packed = pl.pallas_call(
        functools.partial(conv_body, scale),
        out_shape=packed_shape,
        in_specs=[whole()] * 3,
        out_specs=whole(),
        scratch_shapes=[
            pltpu.VMEM((block_len, (spans + 1) * block_len), BF16),
            pltpu.VMEM((spans * 16, 2 * block_len), BF16),
        ],
        compiler_params=params,
        name="conv",
    )(reaches, gain, packed)
    packed = lax.all_to_all(packed, "ctx", 0, 0, tiled=True)
    tap_shape, skip_shape = (local_groups, block_len), (1, local_width)
    mixed, query_grad, key_grad, value_grad, tap_grad, skip_grad = pl.pallas_call(
        functools.partial(gate_body, scale),
        out_shape=(act,) * 4
        + (jax.ShapeDtypeStruct(tap_shape, F32), jax.ShapeDtypeStruct(skip_shape, F32)),
        in_specs=[whole()] * 5,
        out_specs=[whole(pltpu.HBM)] * 6,
        scratch_shapes=[act_buf] * 4
        + [pltpu.VMEM(tap_shape, F32), pltpu.VMEM(skip_shape, F32), pltpu.SemaphoreType.DMA((6,))],
        compiler_params=params,
        name="gate",
    )(query_seq, key_seq, value_seq, out_grad, packed)
    return (mixed, query_grad, key_grad, value_grad, tap_grad.T, skip_grad[0])


def solution(mesh):
    spec = P("ctx", "ch")
    return jax.shard_map(
        body,
        mesh=mesh,
        in_specs=(spec, spec, spec, spec, spec, P("ch"), P("ch")),
        out_specs=(spec, spec, spec, spec, spec, P("ch")),
        check_vma=False,
    )
```

```python
import functools
import math

import jax
import jax.numpy as jnp
from jax import lax
from jax.experimental import pallas as pl
from jax.experimental.pallas import tpu as pltpu
from jax.sharding import PartitionSpec as P

GROUP = 16
OWN = 8
ROWS = 2 * OWN + 2
F32 = jnp.float32
BF16 = jnp.bfloat16


def eye(size, flip):
    row = lax.broadcasted_iota(jnp.int32, (size, size), 0)
    col = lax.broadcasted_iota(jnp.int32, (size, size), 1)
    hit = (row + col == size - 1) if flip else (row == col)
    return jnp.where(hit, 1.0, 0.0).astype(BF16)


def matmul(lhs, rhs):
    return jnp.dot(lhs, rhs, preferred_element_type=F32)


def matmul_nt(lhs, rhs):
    return lax.dot_general(lhs, rhs, (((1,), (1,)), ((), ())), preferred_element_type=F32)


def product(first, second):
    return (first.astype(F32) * second.astype(F32)).astype(BF16)


def pack_body(query, key, value, cotangent, taps, gain, reaches, packed, gain_out, reach_out, q_buf, k_buf, v_buf, o_buf, t_buf, sems):
    spans = packed.shape[0] // ROWS
    moves = [
        pltpu.make_async_copy(source, target, sems.at[place])
        for place, (source, target) in enumerate(
            [
                (key, k_buf),
                (value, v_buf),
                (cotangent, o_buf),
                (query, q_buf),
                (taps, t_buf),
                (gain, gain_out),
                (reaches, reach_out),
            ]
        )
    ]
    for move in moves:
        move.start()
    moves[0].wait()
    moves[1].wait()
    z_rows = product(k_buf[...], v_buf[...]).astype(F32).T
    moves[2].wait()
    moves[3].wait()
    g_rows = product(o_buf[...], q_buf[...]).astype(F32).T
    moves[4].wait()
    tap_rows = t_buf[...].astype(F32)
    for dest in range(spans):
        here = slice(dest * OWN, (dest + 1) * OWN)
        base = dest * ROWS
        tile = jnp.concatenate([z_rows[here], g_rows[here]], axis=0)
        packed[base : base + 2 * OWN] = tile.astype(BF16)
        group = dest * OWN // GROUP
        tail = jnp.broadcast_to(tap_rows[group : group + 1], (2, tap_rows.shape[1]))
        packed[base + 2 * OWN : base + ROWS] = tail.astype(BF16)
    moves[5].wait()
    moves[6].wait()


def conv_body(scale, reaches, gain, packed, out, toep, shifted):
    spans, block_len = packed.shape[0] // ROWS, packed.shape[1]
    wide = 2 * block_len
    half = spans // 2
    owner = lax.axis_index("ctx")
    place = lax.broadcasted_iota(jnp.int32, (1, reaches.shape[1]), 1)
    reach = jnp.sum(jnp.where(place == owner * 8 // GROUP, reaches[...].astype(F32), 0.0), axis=1, keepdims=True)
    place = lax.broadcasted_iota(jnp.int32, (8, gain.shape[1]), 1)
    channel = lax.broadcasted_iota(jnp.int32, (8, gain.shape[1]), 0) + owner * 8
    own_gain = jnp.sum(jnp.where(place == channel, gain[...], 0.0), axis=1, keepdims=True)
    row = lax.broadcasted_iota(jnp.int32, (block_len, block_len), 0)
    col = lax.broadcasted_iota(jnp.int32, (block_len, block_len), 1)
    upper = col >= row
    flip = eye(block_len, True)

    tiles = [packed[span * ROWS : span * ROWS + 2 * OWN].astype(F32) for span in range(spans)]
    z_list = [tile[:OWN] for tile in tiles]
    g_list = [tile[OWN:] for tile in tiles]
    taps = [packed[(span + 1) * ROWS - 2 : (span + 1) * ROWS].astype(F32)[:1] for span in range(spans)]
    reach = jnp.broadcast_to(reach, (8, block_len))
    weights = [
        jnp.concatenate([jnp.where(reach > offset, 1.0, 0.0)] * (block_len // 8), axis=0)
        for offset in range(spans)
    ]

    toep[:, 0:block_len] = jnp.zeros((block_len, block_len), BF16)
    before = jnp.zeros((block_len, block_len), F32)
    for offset in range(spans):
        window = jnp.broadcast_to(taps[offset], (block_len, block_len))
        turned = pltpu.roll(window, 0, 1, stride=1, stride_axis=0)
        block = jnp.where(upper, turned, before) * weights[offset]
        toep[:, (offset + 1) * block_len : (offset + 2) * block_len] = block.astype(BF16)
        before = turned

    g_all = jnp.concatenate(g_list, axis=0).astype(BF16)
    g_flip = matmul(g_all, flip)

    parts = []
    for pair in range(half):
        first = 2 * pair
        parts.append(jnp.concatenate([z_list[first], z_list[first + 1]], axis=1))
        low, high = (spans - 1 - first) * 8, (spans - 2 - first) * 8
        parts.append(jnp.concatenate([g_flip[low : low + 8], g_flip[high : high + 8]], axis=1))
    data = jnp.concatenate(parts, axis=0).astype(BF16)
    acc = None
    for offset in range(half):
        base = 2 * offset * block_len
        block = jnp.concatenate(
            [toep[:, base + block_len : base + block_len + wide], toep[:, base : base + wide]], axis=0
        )
        term = matmul(data[: (half - offset) * 16], block)
        if acc is None:
            acc = term
        else:
            acc = jnp.concatenate([acc[: offset * 16], acc[offset * 16 :] + term], axis=0)

    z_flip = matmul(jnp.concatenate(z_list, axis=0).astype(BF16), flip)
    z_down = jnp.concatenate([jnp.zeros((8, block_len), F32), z_flip[:-8]], axis=0)
    shifted[0 : spans * 8] = jnp.zeros((spans * 8, wide), BF16)
    shifted[spans * 8 : spans * 16] = jnp.concatenate([z_flip, z_down], axis=1).astype(BF16)
    g_turn = jnp.concatenate(g_list, axis=0).T.astype(BF16)
    turned = []
    for pair in range(half):
        start = spans * 8 - 16 * pair
        prods = matmul(g_turn, shifted[start : start + spans * 8])
        for side in range(2):
            own = prods[:, side * block_len : (side + 1) * block_len] * weights[2 * pair + side]
            turned.append(pltpu.roll(own, 1, 1, stride=1, stride_axis=0))
    turned.append(jnp.zeros((block_len, block_len), F32))

    skip = jnp.zeros((8, block_len), F32)
    for span in range(spans):
        skip = skip + z_list[span] * g_list[span]
    skip = jnp.sum(skip, axis=1, keepdims=True)
    lane = lax.broadcasted_iota(jnp.int32, (8, block_len), 1)
    sub = lax.broadcasted_iota(jnp.int32, (8, block_len), 0)
    skip_row = jnp.sum(jnp.where(lane % 8 == sub, skip, 0.0), axis=0, keepdims=True)
    high = skip_row.astype(BF16).astype(F32)
    skip_row = jnp.where(lane[:1] < block_len // 2, high, skip_row - high)

    for span in range(spans):
        pair, side = span // 2, span % 2
        forth = acc[pair * 16 : pair * 16 + 8, side * block_len : (side + 1) * block_len]
        mirror = spans - 1 - span
        pair, side = mirror // 2, mirror % 2
        back = acc[pair * 16 + 8 : pair * 16 + 16, side * block_len : (side + 1) * block_len]
        sums = jnp.sum(jnp.where(col <= row, turned[span], turned[span + 1]), axis=0, keepdims=True)
        forth = forth * scale + own_gain * z_list[span]
        back = back * scale + own_gain * g_flip[span * 8 : span * 8 + 8]
        base = span * ROWS
        out[base : base + 2 * OWN] = jnp.concatenate([forth, back], axis=0).astype(BF16)
        out[base + 2 * OWN : base + ROWS] = jnp.concatenate([sums, skip_row], axis=0).astype(BF16)


def gate_body(scale, query, key, value, cotangent, packed, mixed, query_grad, key_grad, value_grad, tap_grad, skip_grad, q_buf, o_buf, k_buf, v_buf, t_buf, s_buf, sems):
    spans, block_len = packed.shape[0] // ROWS, packed.shape[1]
    moves = []

    def send(source, target):
        moves.append(pltpu.make_async_copy(source, target, sems.at[len(moves)]))
        moves[-1].start()

    tiles = [packed[span * ROWS : span * ROWS + 2 * OWN].astype(F32) for span in range(spans)]
    tails = [packed[(span + 1) * ROWS - 2 : (span + 1) * ROWS].astype(F32) for span in range(spans)]
    forth = jnp.concatenate([tile[0:8] for tile in tiles], axis=0).astype(BF16)
    total = matmul_nt(eye(block_len, False), forth)
    q_buf[...] = (query[...].astype(F32) * total).astype(BF16)
    send(q_buf, mixed)
    o_buf[...] = (cotangent[...].astype(F32) * total).astype(BF16)
    send(o_buf, query_grad)
    back = jnp.concatenate([tile[8:16] for tile in tiles], axis=0).astype(BF16)
    total = matmul_nt(eye(block_len, True), back)
    k_buf[...] = (value[...].astype(F32) * total).astype(BF16)
    send(k_buf, key_grad)
    v_buf[...] = (key[...].astype(F32) * total).astype(BF16)
    send(v_buf, value_grad)

    per_group = GROUP // 8
    for group in range(spans // per_group):
        line = jnp.zeros((1, block_len), F32)
        for member in range(per_group):
            line = line + tails[group * per_group + member][0:1]
        t_buf[group : group + 1] = line * scale
    send(t_buf, tap_grad)

    lane = lax.broadcasted_iota(jnp.int32, (1, block_len), 1)
    per_row = block_len // OWN
    for part in range(s_buf.shape[1] // block_len):
        line = jnp.zeros((1, block_len), F32)
        other = jnp.zeros((1, block_len), F32)
        for place in range(per_row):
            piece = tails[part * per_row + place][1:2]
            line = jnp.where(lane // OWN == place, piece, line)
            other = jnp.where(lane // OWN == (place + per_row // 2) % per_row, piece, other)
        line = line + pltpu.roll(other, block_len // 2, 1)
        s_buf[:, part * block_len : (part + 1) * block_len] = line
    send(s_buf, skip_grad)
    for move in moves:
        move.wait()


def whole(space=pltpu.VMEM):
    return pl.BlockSpec(memory_space=space)


PARAMS = pltpu.CompilerParams(vmem_limit_bytes=48 * 1024 * 1024)


def pack(query_seq, key_seq, value_seq, out_grad, taps, gain, reaches, spans):
    block_len, width = query_seq.shape
    act_buf = pltpu.VMEM((block_len, width), BF16)
    sources = [query_seq, key_seq, value_seq, out_grad, taps, gain, reaches]
    return pl.pallas_call(
        pack_body,
        out_shape=(
            jax.ShapeDtypeStruct((spans * ROWS, block_len), BF16),
            jax.ShapeDtypeStruct(gain.shape, gain.dtype),
            jax.ShapeDtypeStruct(reaches.shape, reaches.dtype),
        ),
        in_specs=[whole(pltpu.HBM)] * 7,
        out_specs=[whole()] * 3,
        scratch_shapes=[act_buf] * 4 + [pltpu.VMEM(taps.shape, BF16), pltpu.SemaphoreType.DMA((7,))],
        compiler_params=PARAMS,
        name="pack",
    )(*[pltpu.with_memory_space_constraint(x, pltpu.HBM) for x in sources])


def conv(reaches, gain, packed, scale):
    spans, block_len = packed.shape[0] // ROWS, packed.shape[1]
    return pl.pallas_call(
        functools.partial(conv_body, scale),
        out_shape=jax.ShapeDtypeStruct(packed.shape, BF16),
        in_specs=[whole()] * 3,
        out_specs=whole(),
        scratch_shapes=[
            pltpu.VMEM((block_len, (spans + 1) * block_len), BF16),
            pltpu.VMEM((spans * 16, 2 * block_len), BF16),
        ],
        compiler_params=PARAMS,
        name="conv",
    )(reaches, gain, packed)


def gate(query_seq, key_seq, value_seq, out_grad, packed, scale):
    block_len, width = query_seq.shape
    act = jax.ShapeDtypeStruct((block_len, width), BF16)
    act_buf = pltpu.VMEM((block_len, width), BF16)
    tap_shape, skip_shape = (width // GROUP, block_len), (1, width)
    return pl.pallas_call(
        functools.partial(gate_body, scale),
        out_shape=(act,) * 4
        + (jax.ShapeDtypeStruct(tap_shape, F32), jax.ShapeDtypeStruct(skip_shape, F32)),
        in_specs=[whole()] * 5,
        out_specs=[whole(pltpu.HBM)] * 6,
        scratch_shapes=[act_buf] * 4
        + [pltpu.VMEM(tap_shape, F32), pltpu.VMEM(skip_shape, F32), pltpu.SemaphoreType.DMA((6,))],
        compiler_params=PARAMS,
        name="gate",
    )(query_seq, key_seq, value_seq, out_grad, packed)


def exchange(packed, spans):
    paired = packed.reshape(spans, ROWS // 2, 2, packed.shape[1])
    return lax.all_to_all(paired, "ctx", 0, 0, tiled=True).reshape(packed.shape)


def body(query_seq, key_seq, value_seq, out_grad, filters, skip_gain, reaches):
    spans = lax.axis_size("ctx")
    scale = 1.0 / math.sqrt(query_seq.shape[0] * spans)
    acts = (query_seq, key_seq, value_seq, out_grad)
    packed, gain, reaches = pack(*acts, filters.T, skip_gain[None, :], reaches[None, :], spans)
    packed = exchange(packed, spans)
    packed = conv(reaches, gain, packed, scale)
    packed = exchange(packed, spans)
    *grads, tap_grad, skip_grad = gate(*acts, packed, scale)
    return (*grads, tap_grad.T, skip_grad[0])


def solution(mesh):
    spec = P("ctx", "ch")
    return jax.shard_map(
        body,
        mesh=mesh,
        in_specs=(spec, spec, spec, spec, spec, P("ch"), P("ch")),
        out_specs=(spec, spec, spec, spec, spec, P("ch")),
        check_vma=False,
    )
```

```python
import functools
import math

import jax
import jax.numpy as jnp
from jax import lax
from jax.experimental import pallas as pl
from jax.experimental.pallas import tpu as pltpu
from jax.sharding import PartitionSpec as P

GROUP = 16
OWN = 8
ROWS = 2 * OWN + 2
F32 = jnp.float32
BF16 = jnp.bfloat16


def eye(size, flip):
    row = lax.broadcasted_iota(jnp.int32, (size, size), 0)
    col = lax.broadcasted_iota(jnp.int32, (size, size), 1)
    hit = (row + col == size - 1) if flip else (row == col)
    return jnp.where(hit, 1.0, 0.0).astype(BF16)


def matmul(lhs, rhs):
    return jnp.dot(lhs, rhs, preferred_element_type=F32)


def matmul_nt(lhs, rhs):
    return lax.dot_general(lhs, rhs, (((1,), (1,)), ((), ())), preferred_element_type=F32)


def product(first, second):
    return (first.astype(F32) * second.astype(F32)).astype(BF16)


def pack_body(query, key, value, cotangent, taps, gain, reaches, packed, gain_out, reach_out, q_buf, k_buf, v_buf, o_buf, t_buf, sems):
    spans = packed.shape[0] // ROWS
    moves = [
        pltpu.make_async_copy(source, target, sems.at[place])
        for place, (source, target) in enumerate(
            [
                (key, k_buf),
                (value, v_buf),
                (cotangent, o_buf),
                (query, q_buf),
                (taps, t_buf),
                (gain, gain_out),
                (reaches, reach_out),
            ]
        )
    ]
    for place in (0, 1, 4, 2, 3, 5, 6):
        moves[place].start()
    moves[0].wait()
    moves[1].wait()
    z_rows = product(k_buf[...], v_buf[...]).T.astype(F32)
    moves[4].wait()
    tap_rows = t_buf[...].astype(F32)
    for dest in range(spans):
        base = dest * ROWS
        group = dest * OWN // GROUP
        tail = jnp.broadcast_to(tap_rows[group : group + 1], (2, tap_rows.shape[1]))
        packed[base + 2 * OWN : base + ROWS] = tail.astype(BF16)
    moves[2].wait()
    moves[3].wait()
    g_rows = product(o_buf[...], q_buf[...]).T.astype(F32)
    for dest in range(spans):
        here = slice(dest * OWN, (dest + 1) * OWN)
        base = dest * ROWS
        tile = jnp.concatenate([z_rows[here], g_rows[here]], axis=0)
        packed[base : base + 2 * OWN] = tile.astype(BF16)
    moves[5].wait()
    moves[6].wait()


def conv_body(scale, reaches, gain, packed, out, toep, shifted, acc_ref):
    spans, block_len = packed.shape[0] // ROWS, packed.shape[1]
    wide = 2 * block_len
    half = spans // 2
    owner = lax.axis_index("ctx")
    place = lax.broadcasted_iota(jnp.int32, (1, reaches.shape[1]), 1)
    reach = jnp.sum(jnp.where(place == owner * 8 // GROUP, reaches[...].astype(F32), 0.0), axis=1, keepdims=True)
    place = lax.broadcasted_iota(jnp.int32, (8, gain.shape[1]), 1)
    channel = lax.broadcasted_iota(jnp.int32, (8, gain.shape[1]), 0) + owner * 8
    own_gain = jnp.sum(jnp.where(place == channel, gain[...], 0.0), axis=1, keepdims=True)
    row = lax.broadcasted_iota(jnp.int32, (block_len, block_len), 0)
    col = lax.broadcasted_iota(jnp.int32, (block_len, block_len), 1)
    upper = col >= row
    flip = eye(block_len, True)

    tiles = [packed[span * ROWS : span * ROWS + 2 * OWN].astype(F32) for span in range(spans)]
    z_list = [tile[:OWN] for tile in tiles]
    g_list = [tile[OWN:] for tile in tiles]
    taps = [packed[(span + 1) * ROWS - 2 : (span + 1) * ROWS].astype(F32)[:1] for span in range(spans)]
    reach = jnp.broadcast_to(reach, (8, block_len))
    weights = [
        jnp.concatenate([jnp.where(reach > offset, 1.0, 0.0)] * (block_len // 8), axis=0)
        for offset in range(spans)
    ]

    g_all = jnp.concatenate(g_list, axis=0).astype(BF16)
    g_flip = matmul(g_all, flip)
    z_flip = matmul(jnp.concatenate(z_list, axis=0).astype(BF16), flip)
    z_down = jnp.concatenate([jnp.zeros((8, block_len), F32), z_flip[:-8]], axis=0)
    shifted[0 : spans * 8] = jnp.zeros((spans * 8, wide), BF16)
    shifted[spans * 8 : spans * 16] = jnp.concatenate([z_flip, z_down], axis=1).astype(BF16)
    g_turn = jnp.concatenate(g_list, axis=0).T.astype(BF16)
    parts = []
    for pair in range(half):
        first = 2 * pair
        parts.append(jnp.concatenate([z_list[first], z_list[first + 1]], axis=1))
        low, high = (spans - 1 - first) * 8, (spans - 2 - first) * 8
        parts.append(jnp.concatenate([g_flip[low : low + 8], g_flip[high : high + 8]], axis=1))
    data = jnp.concatenate(parts, axis=0).astype(BF16)

    toep[:, 0:block_len] = jnp.zeros((block_len, block_len), BF16)
    before = jnp.zeros((block_len, block_len), F32)
    acc = None
    sum_rows = []
    last = None
    for pair in range(half):
        for offset in (2 * pair, 2 * pair + 1):
            window = jnp.broadcast_to(taps[offset], (block_len, block_len))
            turned = pltpu.roll(window, 0, 1, stride=1, stride_axis=0)
            block = jnp.where(col >= row, turned, before)
            toep[:, (offset + 1) * block_len : (offset + 2) * block_len] = block.astype(BF16) * weights[offset].astype(BF16)
            before = turned
        base = 2 * pair * block_len
        block = jnp.concatenate(
            [toep[:, base + block_len : base + block_len + wide], toep[:, base : base + wide]], axis=0
        )
        term = matmul(data[: (half - pair) * 16], block)
        if acc is None:
            acc = acc_ref
            acc[...] = term
        else:
            acc[pair * 16 :] += term
        start = spans * 8 - 16 * pair
        prods = matmul(g_turn, shifted[start : start + spans * 8])
        for side in range(2):
            own = prods[:, side * block_len : (side + 1) * block_len] * weights[2 * pair + side]
            own = pltpu.roll(own, 1, 1, stride=1, stride_axis=0)
            if last is not None:
                sum_rows.append(jnp.sum(jnp.where(col <= row, last, own), axis=0, keepdims=True))
            last = own
    sum_rows.append(jnp.sum(jnp.where(col <= row, last, 0.0), axis=0, keepdims=True))

    skip = jnp.zeros((8, block_len), F32)
    for span in range(spans):
        skip = skip + z_list[span] * g_list[span]
    skip = jnp.sum(skip, axis=1, keepdims=True)
    lane = lax.broadcasted_iota(jnp.int32, (8, block_len), 1)
    sub = lax.broadcasted_iota(jnp.int32, (8, block_len), 0)
    skip_row = jnp.sum(jnp.where(lane % 8 == sub, skip, 0.0), axis=0, keepdims=True)
    high = skip_row.astype(BF16).astype(F32)
    skip_row = jnp.where(lane[:1] < block_len // 2, high, skip_row - high)

    for span in range(spans):
        pair, side = span // 2, span % 2
        forth = acc[pair * 16 : pair * 16 + 8, side * block_len : (side + 1) * block_len]
        mirror = spans - 1 - span
        pair, side = mirror // 2, mirror % 2
        back = acc[pair * 16 + 8 : pair * 16 + 16, side * block_len : (side + 1) * block_len]
        sums = sum_rows[span]
        forth = forth * scale + own_gain * z_list[span]
        back = back * scale + own_gain * g_flip[span * 8 : span * 8 + 8]
        base = span * ROWS
        out[base : base + 2 * OWN] = jnp.concatenate([forth, back], axis=0).astype(BF16)
        out[base + 2 * OWN : base + ROWS] = jnp.concatenate([sums, skip_row], axis=0).astype(BF16)


def gate_body(scale, query, key, value, cotangent, packed, mixed, query_grad, key_grad, value_grad, tap_grad, skip_grad, q_buf, o_buf, k_buf, v_buf, t_buf, s_buf, sems):
    spans, block_len = packed.shape[0] // ROWS, packed.shape[1]
    moves = []

    def send(source, target):
        moves.append(pltpu.make_async_copy(source, target, sems.at[len(moves)]))
        moves[-1].start()

    tiles = [packed[span * ROWS : span * ROWS + 2 * OWN].astype(F32) for span in range(spans)]
    tails = [packed[(span + 1) * ROWS - 2 : (span + 1) * ROWS].astype(F32) for span in range(spans)]
    total = jnp.concatenate([tile[:OWN] for tile in tiles], axis=0).T
    q_buf[...] = (query[...].astype(F32) * total).astype(BF16)
    send(q_buf, mixed)
    o_buf[...] = (cotangent[...].astype(F32) * total).astype(BF16)
    send(o_buf, query_grad)
    back = jnp.concatenate([tile[OWN:] for tile in tiles], axis=0).astype(BF16)
    total = matmul_nt(eye(block_len, True), back)
    k_buf[...] = (value[...].astype(F32) * total).astype(BF16)
    send(k_buf, key_grad)
    v_buf[...] = (key[...].astype(F32) * total).astype(BF16)
    send(v_buf, value_grad)

    per_group = GROUP // 8
    for group in range(spans // per_group):
        line = jnp.zeros((1, block_len), F32)
        for member in range(per_group):
            line = line + tails[group * per_group + member][0:1]
        t_buf[group : group + 1] = line * scale
    send(t_buf, tap_grad)

    lane = lax.broadcasted_iota(jnp.int32, (1, block_len), 1)
    per_row = block_len // OWN
    for part in range(s_buf.shape[1] // block_len):
        line = jnp.zeros((1, block_len), F32)
        other = jnp.zeros((1, block_len), F32)
        for place in range(per_row):
            piece = tails[part * per_row + place][1:2]
            line = jnp.where(lane // OWN == place, piece, line)
            other = jnp.where(lane // OWN == (place + per_row // 2) % per_row, piece, other)
        line = line + pltpu.roll(other, block_len // 2, 1)
        s_buf[:, part * block_len : (part + 1) * block_len] = line
    send(s_buf, skip_grad)
    for move in moves:
        move.wait()


def whole(space=pltpu.VMEM):
    return pl.BlockSpec(memory_space=space)


PARAMS = pltpu.CompilerParams(vmem_limit_bytes=48 * 1024 * 1024)


def pack(query_seq, key_seq, value_seq, out_grad, taps, gain, reaches, spans):
    block_len, width = query_seq.shape
    act_buf = pltpu.VMEM((block_len, width), BF16)
    sources = [query_seq, key_seq, value_seq, out_grad, taps, gain, reaches]
    return pl.pallas_call(
        pack_body,
        out_shape=(
            jax.ShapeDtypeStruct((spans * ROWS, block_len), BF16),
            jax.ShapeDtypeStruct(gain.shape, gain.dtype),
            jax.ShapeDtypeStruct(reaches.shape, reaches.dtype),
        ),
        in_specs=[whole(pltpu.HBM)] * 7,
        out_specs=[whole()] * 3,
        scratch_shapes=[act_buf] * 4 + [pltpu.VMEM(taps.shape, BF16), pltpu.SemaphoreType.DMA((7,))],
        compiler_params=PARAMS,
        name="pack",
    )(*[pltpu.with_memory_space_constraint(x, pltpu.HBM) for x in sources])


def conv(reaches, gain, packed, scale):
    spans, block_len = packed.shape[0] // ROWS, packed.shape[1]
    return pl.pallas_call(
        functools.partial(conv_body, scale),
        out_shape=jax.ShapeDtypeStruct(packed.shape, BF16),
        in_specs=[whole()] * 3,
        out_specs=whole(),
        scratch_shapes=[
            pltpu.VMEM((block_len, (spans + 1) * block_len), BF16),
            pltpu.VMEM((spans * 16, 2 * block_len), BF16),
            pltpu.VMEM((spans * 8, 2 * block_len), F32),
        ],
        compiler_params=PARAMS,
        name="conv",
    )(reaches, gain, packed)


def gate(query_seq, key_seq, value_seq, out_grad, packed, scale):
    block_len, width = query_seq.shape
    act = jax.ShapeDtypeStruct((block_len, width), BF16)
    act_buf = pltpu.VMEM((block_len, width), BF16)
    tap_shape, skip_shape = (width // GROUP, block_len), (1, width)
    return pl.pallas_call(
        functools.partial(gate_body, scale),
        out_shape=(act,) * 4
        + (jax.ShapeDtypeStruct(tap_shape, F32), jax.ShapeDtypeStruct(skip_shape, F32)),
        in_specs=[whole()] * 5,
        out_specs=[whole(pltpu.HBM)] * 6,
        scratch_shapes=[act_buf] * 4
        + [pltpu.VMEM(tap_shape, F32), pltpu.VMEM(skip_shape, F32), pltpu.SemaphoreType.DMA((6,))],
        compiler_params=PARAMS,
        name="gate",
    )(query_seq, key_seq, value_seq, out_grad, packed)


def exchange(packed, spans):
    paired = packed.reshape(spans, ROWS // 2, 2, packed.shape[1])
    return lax.all_to_all(paired, "ctx", 0, 0, tiled=True).reshape(packed.shape)


def body(query_seq, key_seq, value_seq, out_grad, filters, skip_gain, reaches):
    spans = lax.axis_size("ctx")
    scale = 1.0 / math.sqrt(query_seq.shape[0] * spans)
    acts = (query_seq, key_seq, value_seq, out_grad)
    packed, gain, reaches = pack(*acts, filters.T, skip_gain[None, :], reaches[None, :], spans)
    packed = exchange(packed, spans)
    packed = conv(reaches, gain, packed, scale)
    packed = exchange(packed, spans)
    *grads, tap_grad, skip_grad = gate(*acts, packed, scale)
    return (*grads, tap_grad.T, skip_grad[0])


def solution(mesh):
    spec = P("ctx", "ch")
    return jax.shard_map(
        body,
        mesh=mesh,
        in_specs=(spec, spec, spec, spec, spec, P("ch"), P("ch")),
        out_specs=(spec, spec, spec, spec, spec, P("ch")),
        check_vma=False,
    )
```

```python
import functools
import math

import jax
import jax.numpy as jnp
from jax import lax
from jax.experimental import pallas as pl
from jax.experimental.pallas import tpu as pltpu
from jax.sharding import PartitionSpec as P

GROUP = 16
OWN = 8
ROWS = 2 * OWN + 2
F32 = jnp.float32
BF16 = jnp.bfloat16


def eye(size, flip):
    row = lax.broadcasted_iota(jnp.int32, (size, size), 0)
    col = lax.broadcasted_iota(jnp.int32, (size, size), 1)
    hit = (row + col == size - 1) if flip else (row == col)
    return jnp.where(hit, 1.0, 0.0).astype(BF16)


def matmul(lhs, rhs):
    return jnp.dot(lhs, rhs, preferred_element_type=F32)


def matmul_nt(lhs, rhs):
    return lax.dot_general(lhs, rhs, (((1,), (1,)), ((), ())), preferred_element_type=F32)


def product(first, second):
    return (first.astype(F32) * second.astype(F32)).astype(BF16)


def pack_body(query, key, value, cotangent, taps, gain, reaches, packed, gain_out, reach_out, q_buf, k_buf, v_buf, o_buf, t_buf, sems):
    spans = packed.shape[0] // ROWS
    moves = [
        pltpu.make_async_copy(source, target, sems.at[place])
        for place, (source, target) in enumerate(
            [
                (key, k_buf),
                (value, v_buf),
                (cotangent, o_buf),
                (query, q_buf),
                (taps, t_buf),
                (gain, gain_out),
                (reaches, reach_out),
            ]
        )
    ]
    for place in (0, 1, 4, 2, 3, 5, 6):
        moves[place].start()
    moves[0].wait()
    moves[1].wait()
    z_rows = product(k_buf[...], v_buf[...]).T.astype(F32)
    moves[4].wait()
    tap_rows = t_buf[...].astype(F32)
    for dest in range(spans):
        base = dest * ROWS
        group = dest * OWN // GROUP
        tail = jnp.broadcast_to(tap_rows[group : group + 1], (2, tap_rows.shape[1]))
        packed[base + 2 * OWN : base + ROWS] = tail.astype(BF16)
    moves[2].wait()
    moves[3].wait()
    g_rows = product(o_buf[...], q_buf[...]).T.astype(F32)
    for dest in range(spans):
        here = slice(dest * OWN, (dest + 1) * OWN)
        base = dest * ROWS
        tile = jnp.concatenate([z_rows[here], g_rows[here]], axis=0)
        packed[base : base + 2 * OWN] = tile.astype(BF16)
    moves[5].wait()
    moves[6].wait()


def conv_body(scale, reaches, gain, packed, out, shifted, acc_ref):
    spans, block_len = packed.shape[0] // ROWS, packed.shape[1]
    wide = 2 * block_len
    half = spans // 2
    owner = lax.axis_index("ctx")
    place = lax.broadcasted_iota(jnp.int32, (1, reaches.shape[1]), 1)
    reach = jnp.sum(jnp.where(place == owner * 8 // GROUP, reaches[...].astype(F32), 0.0), axis=1, keepdims=True)
    place = lax.broadcasted_iota(jnp.int32, (8, gain.shape[1]), 1)
    channel = lax.broadcasted_iota(jnp.int32, (8, gain.shape[1]), 0) + owner * 8
    own_gain = jnp.sum(jnp.where(place == channel, gain[...], 0.0), axis=1, keepdims=True)
    row = lax.broadcasted_iota(jnp.int32, (block_len, block_len), 0)
    col = lax.broadcasted_iota(jnp.int32, (block_len, block_len), 1)
    upper = col >= row
    flip = eye(block_len, True)

    tiles = [packed[span * ROWS : span * ROWS + 2 * OWN].astype(F32) for span in range(spans)]
    z_list = [tile[:OWN] for tile in tiles]
    g_list = [tile[OWN:] for tile in tiles]
    taps = [packed[(span + 1) * ROWS - 2 : (span + 1) * ROWS].astype(F32)[:1] for span in range(spans)]
    reach = jnp.broadcast_to(reach, (8, block_len))
    weights = [
        jnp.concatenate([jnp.where(reach > offset, 1.0, 0.0)] * (block_len // 8), axis=0)
        for offset in range(spans)
    ]

    g_all = jnp.concatenate(g_list, axis=0).astype(BF16)
    g_flip = matmul(g_all, flip)
    z_flip = matmul(jnp.concatenate(z_list, axis=0).astype(BF16), flip)
    z_down = jnp.concatenate([jnp.zeros((8, block_len), F32), z_flip[:-8]], axis=0)
    shifted[0 : spans * 8] = jnp.zeros((spans * 8, wide), BF16)
    shifted[spans * 8 : spans * 16] = jnp.concatenate([z_flip, z_down], axis=1).astype(BF16)
    g_turn = jnp.concatenate(g_list, axis=0).T.astype(BF16)
    parts = []
    for pair in range(half):
        first = 2 * pair
        parts.append(jnp.concatenate([z_list[first], z_list[first + 1]], axis=1))
        low, high = (spans - 1 - first) * 8, (spans - 2 - first) * 8
        parts.append(jnp.concatenate([g_flip[low : low + 8], g_flip[high : high + 8]], axis=1))
    data = jnp.concatenate(parts, axis=0).astype(BF16)

    before = jnp.zeros((block_len, block_len), F32)
    odd = jnp.zeros((block_len, block_len), BF16)
    acc = None
    sum_rows = []
    last = None
    for pair in range(half):
        blocks = [odd]
        for offset in (2 * pair, 2 * pair + 1):
            window = jnp.broadcast_to(taps[offset], (block_len, block_len))
            turned = pltpu.roll(window, 0, 1, stride=1, stride_axis=0)
            block = jnp.where(col >= row, turned, before).astype(BF16)
            blocks.append(block * weights[offset].astype(BF16))
            before = turned
        odd = blocks[2]
        block = jnp.concatenate(
            [jnp.concatenate(blocks[1:], axis=1), jnp.concatenate(blocks[:2], axis=1)], axis=0
        )
        term = matmul(data[: (half - pair) * 16], block)
        if acc is None:
            acc = acc_ref
            acc[...] = term
        else:
            acc[pair * 16 :] += term
        start = spans * 8 - 16 * pair
        prods = matmul(g_turn, shifted[start : start + spans * 8])
        for side in range(2):
            own = prods[:, side * block_len : (side + 1) * block_len] * weights[2 * pair + side]
            own = pltpu.roll(own, 1, 1, stride=1, stride_axis=0)
            if last is not None:
                sum_rows.append(jnp.sum(jnp.where(col <= row, last, own), axis=0, keepdims=True))
            last = own
    sum_rows.append(jnp.sum(jnp.where(col <= row, last, 0.0), axis=0, keepdims=True))

    skip = jnp.zeros((8, block_len), F32)
    for span in range(spans):
        skip = skip + z_list[span] * g_list[span]
    skip = jnp.sum(skip, axis=1, keepdims=True)
    lane = lax.broadcasted_iota(jnp.int32, (8, block_len), 1)
    sub = lax.broadcasted_iota(jnp.int32, (8, block_len), 0)
    skip_row = jnp.sum(jnp.where(lane % 8 == sub, skip, 0.0), axis=0, keepdims=True)
    high = skip_row.astype(BF16).astype(F32)
    skip_row = jnp.where(lane[:1] < block_len // 2, high, skip_row - high)

    for span in range(spans):
        pair, side = span // 2, span % 2
        forth = acc[pair * 16 : pair * 16 + 8, side * block_len : (side + 1) * block_len]
        mirror = spans - 1 - span
        pair, side = mirror // 2, mirror % 2
        back = acc[pair * 16 + 8 : pair * 16 + 16, side * block_len : (side + 1) * block_len]
        sums = sum_rows[span]
        forth = forth * scale + own_gain * z_list[span]
        back = back * scale + own_gain * g_flip[span * 8 : span * 8 + 8]
        base = span * ROWS
        out[base : base + 2 * OWN] = jnp.concatenate([forth, back], axis=0).astype(BF16)
        out[base + 2 * OWN : base + ROWS] = jnp.concatenate([sums, skip_row], axis=0).astype(BF16)


def gate_body(scale, query, key, value, cotangent, packed, mixed, query_grad, key_grad, value_grad, tap_grad, skip_grad, q_buf, o_buf, k_buf, v_buf, t_buf, s_buf, sems):
    spans, block_len = packed.shape[0] // ROWS, packed.shape[1]
    moves = []

    def send(source, target):
        moves.append(pltpu.make_async_copy(source, target, sems.at[len(moves)]))
        moves[-1].start()

    tiles = [packed[span * ROWS : span * ROWS + 2 * OWN].astype(F32) for span in range(spans)]
    tails = [packed[(span + 1) * ROWS - 2 : (span + 1) * ROWS].astype(F32) for span in range(spans)]
    total = jnp.concatenate([tile[:OWN] for tile in tiles], axis=0).T
    q_buf[...] = (query[...].astype(F32) * total).astype(BF16)
    send(q_buf, mixed)
    o_buf[...] = (cotangent[...].astype(F32) * total).astype(BF16)
    send(o_buf, query_grad)
    back = jnp.concatenate([tile[OWN:] for tile in tiles], axis=0).astype(BF16)
    total = matmul_nt(eye(block_len, True), back)
    k_buf[...] = (value[...].astype(F32) * total).astype(BF16)
    send(k_buf, key_grad)
    v_buf[...] = (key[...].astype(F32) * total).astype(BF16)
    send(v_buf, value_grad)

    per_group = GROUP // 8
    for group in range(spans // per_group):
        line = jnp.zeros((1, block_len), F32)
        for member in range(per_group):
            line = line + tails[group * per_group + member][0:1]
        t_buf[group : group + 1] = line * scale
    send(t_buf, tap_grad)

    lane = lax.broadcasted_iota(jnp.int32, (1, block_len), 1)
    per_row = block_len // OWN
    for part in range(s_buf.shape[1] // block_len):
        line = jnp.zeros((1, block_len), F32)
        other = jnp.zeros((1, block_len), F32)
        for place in range(per_row):
            piece = tails[part * per_row + place][1:2]
            line = jnp.where(lane // OWN == place, piece, line)
            other = jnp.where(lane // OWN == (place + per_row // 2) % per_row, piece, other)
        line = line + pltpu.roll(other, block_len // 2, 1)
        s_buf[:, part * block_len : (part + 1) * block_len] = line
    send(s_buf, skip_grad)
    for move in moves:
        move.wait()


def whole(space=pltpu.VMEM):
    return pl.BlockSpec(memory_space=space)


PARAMS = pltpu.CompilerParams(vmem_limit_bytes=48 * 1024 * 1024)


def pack(query_seq, key_seq, value_seq, out_grad, taps, gain, reaches, spans):
    block_len, width = query_seq.shape
    sources = [query_seq, key_seq, value_seq, out_grad, taps, gain, reaches]
    return pl.pallas_call(
        pack_body,
        out_shape=(
            jax.ShapeDtypeStruct((spans * ROWS, block_len), BF16),
            jax.ShapeDtypeStruct(gain.shape, gain.dtype),
            jax.ShapeDtypeStruct(reaches.shape, reaches.dtype),
        )
        + (jax.ShapeDtypeStruct((block_len, width), BF16),) * 4,
        in_specs=[whole(pltpu.HBM)] * 7,
        out_specs=[whole()] * 7,
        scratch_shapes=[pltpu.VMEM(taps.shape, BF16), pltpu.SemaphoreType.DMA((7,))],
        compiler_params=PARAMS,
        name="pack",
    )(*[pltpu.with_memory_space_constraint(x, pltpu.HBM) for x in sources])


def conv(reaches, gain, packed, scale):
    spans, block_len = packed.shape[0] // ROWS, packed.shape[1]
    return pl.pallas_call(
        functools.partial(conv_body, scale),
        out_shape=jax.ShapeDtypeStruct(packed.shape, BF16),
        in_specs=[whole()] * 3,
        out_specs=whole(),
        scratch_shapes=[
            pltpu.VMEM((spans * 16, 2 * block_len), BF16),
            pltpu.VMEM((spans * 8, 2 * block_len), F32),
        ],
        compiler_params=PARAMS,
        name="conv",
    )(reaches, gain, packed)


def gate(query_seq, key_seq, value_seq, out_grad, packed, scale):
    block_len, width = query_seq.shape
    act = jax.ShapeDtypeStruct((block_len, width), BF16)
    act_buf = pltpu.VMEM((block_len, width), BF16)
    tap_shape, skip_shape = (width // GROUP, block_len), (1, width)
    return pl.pallas_call(
        functools.partial(gate_body, scale),
        out_shape=(act,) * 4
        + (jax.ShapeDtypeStruct(tap_shape, F32), jax.ShapeDtypeStruct(skip_shape, F32)),
        in_specs=[whole()] * 5,
        out_specs=[whole(pltpu.HBM)] * 6,
        scratch_shapes=[act_buf] * 4
        + [pltpu.VMEM(tap_shape, F32), pltpu.VMEM(skip_shape, F32), pltpu.SemaphoreType.DMA((6,))],
        compiler_params=PARAMS,
        name="gate",
    )(query_seq, key_seq, value_seq, out_grad, packed)


def exchange(packed, spans):
    paired = packed.reshape(spans, ROWS // 2, 2, packed.shape[1])
    return lax.all_to_all(paired, "ctx", 0, 0, tiled=True).reshape(packed.shape)


def body(query_seq, key_seq, value_seq, out_grad, filters, skip_gain, reaches):
    spans = lax.axis_size("ctx")
    scale = 1.0 / math.sqrt(query_seq.shape[0] * spans)
    acts = (query_seq, key_seq, value_seq, out_grad)
    packed, gain, reaches, *acts = pack(*acts, filters.T, skip_gain[None, :], reaches[None, :], spans)
    packed = exchange(packed, spans)
    packed = conv(reaches, gain, packed, scale)
    packed = exchange(packed, spans)
    *grads, tap_grad, skip_grad = gate(*acts, packed, scale)
    return (*grads, tap_grad.T, skip_grad[0])


def solution(mesh):
    spec = P("ctx", "ch")
    return jax.shard_map(
        body,
        mesh=mesh,
        in_specs=(spec, spec, spec, spec, spec, P("ch"), P("ch")),
        out_specs=(spec, spec, spec, spec, spec, P("ch")),
        check_vma=False,
    )
```

```python
import functools
import math

import jax
import jax.numpy as jnp
from jax import lax
from jax.experimental import pallas as pl
from jax.experimental.pallas import tpu as pltpu
from jax.sharding import PartitionSpec as P

GROUP = 16
OWN = 8
ROWS = 2 * OWN + 2
F32 = jnp.float32
BF16 = jnp.bfloat16


def eye(size, flip):
    row = lax.broadcasted_iota(jnp.int32, (size, size), 0)
    col = lax.broadcasted_iota(jnp.int32, (size, size), 1)
    hit = (row + col == size - 1) if flip else (row == col)
    return jnp.where(hit, 1.0, 0.0).astype(BF16)


def matmul(lhs, rhs):
    return jnp.dot(lhs, rhs, preferred_element_type=F32)


def matmul_nt(lhs, rhs):
    return lax.dot_general(lhs, rhs, (((1,), (1,)), ((), ())), preferred_element_type=F32)


def product(first, second):
    return (first.astype(F32) * second.astype(F32)).astype(BF16)


def pack_body(query, key, value, cotangent, taps, gain, reaches, packed, gain_out, reach_out, q_buf, k_buf, v_buf, o_buf, t_buf, sems):
    spans = packed.shape[0] // ROWS
    moves = [
        pltpu.make_async_copy(source, target, sems.at[place])
        for place, (source, target) in enumerate(
            [
                (key, k_buf),
                (value, v_buf),
                (cotangent, o_buf),
                (query, q_buf),
                (taps, t_buf),
                (gain, gain_out),
                (reaches, reach_out),
            ]
        )
    ]
    for place in (0, 1, 4, 2, 3, 5, 6):
        moves[place].start()
    moves[0].wait()
    moves[1].wait()
    z_rows = product(k_buf[...], v_buf[...]).T.astype(F32)
    moves[4].wait()
    tap_rows = t_buf[...].astype(F32)
    for dest in range(spans):
        base = dest * ROWS
        group = dest * OWN // GROUP
        tail = jnp.broadcast_to(tap_rows[group : group + 1], (2, tap_rows.shape[1]))
        packed[base + 2 * OWN : base + ROWS] = tail.astype(BF16)
    moves[2].wait()
    moves[3].wait()
    g_rows = product(o_buf[...], q_buf[...]).T.astype(F32)
    for dest in range(spans):
        here = slice(dest * OWN, (dest + 1) * OWN)
        base = dest * ROWS
        tile = jnp.concatenate([z_rows[here], g_rows[here]], axis=0)
        packed[base : base + 2 * OWN] = tile.astype(BF16)
    moves[5].wait()
    moves[6].wait()


def conv_body(scale, reaches, gain, packed, out, shifted, acc_ref):
    spans, block_len = packed.shape[0] // ROWS, packed.shape[1]
    wide = 2 * block_len
    half = spans // 2
    owner = lax.axis_index("ctx")
    place = lax.broadcasted_iota(jnp.int32, (1, reaches.shape[1]), 1)
    reach = jnp.sum(jnp.where(place == owner * 8 // GROUP, reaches[...].astype(F32), 0.0), axis=1, keepdims=True)
    place = lax.broadcasted_iota(jnp.int32, (8, gain.shape[1]), 1)
    channel = lax.broadcasted_iota(jnp.int32, (8, gain.shape[1]), 0) + owner * 8
    own_gain = jnp.sum(jnp.where(place == channel, gain[...], 0.0), axis=1, keepdims=True)
    row = lax.broadcasted_iota(jnp.int32, (block_len, block_len), 0)
    col = lax.broadcasted_iota(jnp.int32, (block_len, block_len), 1)
    upper = col >= row
    flip = eye(block_len, True)

    tiles = [packed[span * ROWS : span * ROWS + 2 * OWN].astype(F32) for span in range(spans)]
    z_list = [tile[:OWN] for tile in tiles]
    g_list = [tile[OWN:] for tile in tiles]
    taps = [packed[(span + 1) * ROWS - 2 : (span + 1) * ROWS].astype(F32)[:1] for span in range(spans)]
    reach = jnp.broadcast_to(reach, (8, block_len))
    weights = [
        jnp.concatenate([jnp.where(reach > offset, 1.0, 0.0)] * (block_len // 8), axis=0)
        for offset in range(spans)
    ]

    g_all = jnp.concatenate(g_list, axis=0).astype(BF16)
    g_flip = matmul(g_all, flip)
    z_flip = matmul(jnp.concatenate(z_list, axis=0).astype(BF16), flip)
    z_down = jnp.concatenate([jnp.zeros((8, block_len), F32), z_flip[:-8]], axis=0)
    shifted[0 : spans * 8] = jnp.zeros((spans * 8, wide), BF16)
    shifted[spans * 8 : spans * 16] = jnp.concatenate([z_flip, z_down], axis=1).astype(BF16)
    g_turn = jnp.concatenate(g_list, axis=0).T.astype(BF16)
    skip = jnp.zeros((8, block_len), F32)
    for span in range(spans):
        skip = skip + z_list[span] * g_list[span]
    skip = jnp.sum(skip, axis=1, keepdims=True)
    lane = lax.broadcasted_iota(jnp.int32, (8, block_len), 1)
    sub = lax.broadcasted_iota(jnp.int32, (8, block_len), 0)
    skip_row = jnp.sum(jnp.where(lane % 8 == sub, skip, 0.0), axis=0, keepdims=True)
    high = skip_row.astype(BF16).astype(F32)
    skip_row = jnp.where(lane[:1] < block_len // 2, high, skip_row - high)

    parts = []
    for pair in range(half):
        first = 2 * pair
        parts.append(jnp.concatenate([z_list[first], z_list[first + 1]], axis=1))
        low, high = (spans - 1 - first) * 8, (spans - 2 - first) * 8
        parts.append(jnp.concatenate([g_flip[low : low + 8], g_flip[high : high + 8]], axis=1))
    data = jnp.concatenate(parts, axis=0).astype(BF16)

    before = jnp.zeros((block_len, block_len), F32)
    odd = jnp.zeros((block_len, block_len), BF16)
    acc = None
    sum_rows = []
    last = None
    for pair in range(half):
        blocks = [odd]
        for offset in (2 * pair, 2 * pair + 1):
            window = jnp.broadcast_to(taps[offset], (block_len, block_len))
            turned = pltpu.roll(window, 0, 1, stride=1, stride_axis=0)
            block = jnp.where(col >= row, turned, before).astype(BF16)
            blocks.append(block * weights[offset].astype(BF16))
            before = turned
        odd = blocks[2]
        block = jnp.concatenate(
            [jnp.concatenate(blocks[1:], axis=1), jnp.concatenate(blocks[:2], axis=1)], axis=0
        )
        term = matmul(data[: (half - pair) * 16], block)
        if acc is None:
            acc = acc_ref
            acc[...] = term
        else:
            acc[pair * 16 :] += term
        start = spans * 8 - 16 * pair
        prods = matmul(g_turn, shifted[start : start + spans * 8])
        for side in range(2):
            own = prods[:, side * block_len : (side + 1) * block_len] * weights[2 * pair + side]
            own = pltpu.roll(own, 1, 1, stride=1, stride_axis=0)
            if last is not None:
                sum_rows.append(jnp.sum(jnp.where(col <= row, last, own), axis=0, keepdims=True))
            last = own
    sum_rows.append(jnp.sum(jnp.where(col <= row, last, 0.0), axis=0, keepdims=True))

    for span in range(spans):
        pair, side = span // 2, span % 2
        forth = acc[pair * 16 : pair * 16 + 8, side * block_len : (side + 1) * block_len]
        mirror = spans - 1 - span
        pair, side = mirror // 2, mirror % 2
        back = acc[pair * 16 + 8 : pair * 16 + 16, side * block_len : (side + 1) * block_len]
        sums = sum_rows[span]
        forth = forth * scale + own_gain * z_list[span]
        back = back * scale + own_gain * g_flip[span * 8 : span * 8 + 8]
        base = span * ROWS
        out[base : base + 2 * OWN] = jnp.concatenate([forth, back], axis=0).astype(BF16)
        out[base + 2 * OWN : base + ROWS] = jnp.concatenate([sums, skip_row], axis=0).astype(BF16)


def gate_body(scale, query, key, value, cotangent, packed, mixed, query_grad, key_grad, value_grad, tap_grad, skip_grad, q_buf, o_buf, k_buf, v_buf, t_buf, s_buf, sems):
    spans, block_len = packed.shape[0] // ROWS, packed.shape[1]
    moves = []

    def send(source, target):
        moves.append(pltpu.make_async_copy(source, target, sems.at[len(moves)]))
        moves[-1].start()

    tiles = [packed[span * ROWS : span * ROWS + 2 * OWN].astype(F32) for span in range(spans)]
    tails = [packed[(span + 1) * ROWS - 2 : (span + 1) * ROWS].astype(F32) for span in range(spans)]
    total = jnp.concatenate([tile[:OWN] for tile in tiles], axis=0).T
    q_buf[...] = (query[...].astype(F32) * total).astype(BF16)
    send(q_buf, mixed)
    o_buf[...] = (cotangent[...].astype(F32) * total).astype(BF16)
    send(o_buf, query_grad)
    back = jnp.concatenate([tile[OWN:] for tile in tiles], axis=0).astype(BF16)
    total = matmul_nt(eye(block_len, True), back)
    k_buf[...] = (value[...].astype(F32) * total).astype(BF16)
    send(k_buf, key_grad)
    v_buf[...] = (key[...].astype(F32) * total).astype(BF16)
    send(v_buf, value_grad)

    per_group = GROUP // 8
    for group in range(spans // per_group):
        line = jnp.zeros((1, block_len), F32)
        for member in range(per_group):
            line = line + tails[group * per_group + member][0:1]
        t_buf[group : group + 1] = line * scale
    send(t_buf, tap_grad)

    lane = lax.broadcasted_iota(jnp.int32, (1, block_len), 1)
    per_row = block_len // OWN
    for part in range(s_buf.shape[1] // block_len):
        line = jnp.zeros((1, block_len), F32)
        other = jnp.zeros((1, block_len), F32)
        for place in range(per_row):
            piece = tails[part * per_row + place][1:2]
            line = jnp.where(lane // OWN == place, piece, line)
            other = jnp.where(lane // OWN == (place + per_row // 2) % per_row, piece, other)
        line = line + pltpu.roll(other, block_len // 2, 1)
        s_buf[:, part * block_len : (part + 1) * block_len] = line
    send(s_buf, skip_grad)
    for move in moves:
        move.wait()


def whole(space=pltpu.VMEM):
    return pl.BlockSpec(memory_space=space)


PARAMS = pltpu.CompilerParams(vmem_limit_bytes=48 * 1024 * 1024)


def pack(query_seq, key_seq, value_seq, out_grad, taps, gain, reaches, spans):
    block_len, width = query_seq.shape
    sources = [query_seq, key_seq, value_seq, out_grad, taps, gain, reaches]
    return pl.pallas_call(
        pack_body,
        out_shape=(
            jax.ShapeDtypeStruct((spans * ROWS, block_len), BF16),
            jax.ShapeDtypeStruct(gain.shape, gain.dtype),
            jax.ShapeDtypeStruct(reaches.shape, reaches.dtype),
        )
        + (jax.ShapeDtypeStruct((block_len, width), BF16),) * 4,
        in_specs=[whole(pltpu.HBM)] * 7,
        out_specs=[whole()] * 7,
        scratch_shapes=[pltpu.VMEM(taps.shape, BF16), pltpu.SemaphoreType.DMA((7,))],
        compiler_params=PARAMS,
        name="pack",
    )(*[pltpu.with_memory_space_constraint(x, pltpu.HBM) for x in sources])


def conv(reaches, gain, packed, scale):
    spans, block_len = packed.shape[0] // ROWS, packed.shape[1]
    return pl.pallas_call(
        functools.partial(conv_body, scale),
        out_shape=jax.ShapeDtypeStruct(packed.shape, BF16),
        in_specs=[whole()] * 3,
        out_specs=whole(),
        scratch_shapes=[
            pltpu.VMEM((spans * 16, 2 * block_len), BF16),
            pltpu.VMEM((spans * 8, 2 * block_len), F32),
        ],
        compiler_params=PARAMS,
        name="conv",
    )(reaches, gain, packed)


def gate(query_seq, key_seq, value_seq, out_grad, packed, scale):
    block_len, width = query_seq.shape
    act = jax.ShapeDtypeStruct((block_len, width), BF16)
    act_buf = pltpu.VMEM((block_len, width), BF16)
    tap_shape, skip_shape = (width // GROUP, block_len), (1, width)
    return pl.pallas_call(
        functools.partial(gate_body, scale),
        out_shape=(act,) * 4
        + (jax.ShapeDtypeStruct(tap_shape, F32), jax.ShapeDtypeStruct(skip_shape, F32)),
        in_specs=[whole()] * 5,
        out_specs=[whole(pltpu.HBM)] * 6,
        scratch_shapes=[act_buf] * 4
        + [pltpu.VMEM(tap_shape, F32), pltpu.VMEM(skip_shape, F32), pltpu.SemaphoreType.DMA((6,))],
        compiler_params=PARAMS,
        name="gate",
    )(query_seq, key_seq, value_seq, out_grad, packed)


def exchange(packed, spans):
    paired = packed.reshape(spans, ROWS // 2, 2, packed.shape[1])
    return lax.all_to_all(paired, "ctx", 0, 0, tiled=True).reshape(packed.shape)


def body(query_seq, key_seq, value_seq, out_grad, filters, skip_gain, reaches):
    spans = lax.axis_size("ctx")
    scale = 1.0 / math.sqrt(query_seq.shape[0] * spans)
    acts = (query_seq, key_seq, value_seq, out_grad)
    packed, gain, reaches, *acts = pack(*acts, filters.T, skip_gain[None, :], reaches[None, :], spans)
    packed = exchange(packed, spans)
    packed = conv(reaches, gain, packed, scale)
    packed = exchange(packed, spans)
    *grads, tap_grad, skip_grad = gate(*acts, packed, scale)
    return (*grads, tap_grad.T, skip_grad[0])


def solution(mesh):
    spec = P("ctx", "ch")
    return jax.shard_map(
        body,
        mesh=mesh,
        in_specs=(spec, spec, spec, spec, spec, P("ch"), P("ch")),
        out_specs=(spec, spec, spec, spec, spec, P("ch")),
        check_vma=False,
    )
```

```python
import functools
import math

import jax
import jax.numpy as jnp
from jax import lax
from jax.experimental import pallas as pl
from jax.experimental.pallas import tpu as pltpu
from jax.sharding import PartitionSpec as P

GROUP = 16
OWN = 8
ROWS = 2 * OWN + 2
F32 = jnp.float32
BF16 = jnp.bfloat16


def eye(size, flip):
    row = lax.broadcasted_iota(jnp.int32, (size, size), 0)
    col = lax.broadcasted_iota(jnp.int32, (size, size), 1)
    hit = (row + col == size - 1) if flip else (row == col)
    return jnp.where(hit, 1.0, 0.0).astype(BF16)


def matmul(lhs, rhs):
    return jnp.dot(lhs, rhs, preferred_element_type=F32)


def matmul_nt(lhs, rhs):
    return lax.dot_general(lhs, rhs, (((1,), (1,)), ((), ())), preferred_element_type=F32)


def product(first, second):
    return (first.astype(F32) * second.astype(F32)).astype(BF16)


def pack_body(query, key, value, cotangent, taps, gain, reaches, packed, gain_out, reach_out, q_buf, k_buf, v_buf, o_buf, t_buf, sems):
    spans = packed.shape[0] // ROWS
    moves = [
        pltpu.make_async_copy(source, target, sems.at[place])
        for place, (source, target) in enumerate(
            [
                (key, k_buf),
                (value, v_buf),
                (cotangent, o_buf),
                (query, q_buf),
                (taps, t_buf),
                (gain, gain_out),
                (reaches, reach_out),
            ]
        )
    ]
    for place in (0, 1, 4, 2, 3, 5, 6):
        moves[place].start()
    moves[0].wait()
    moves[1].wait()
    z_rows = product(k_buf[...], v_buf[...]).T.astype(F32)
    for dest in range(spans):
        packed[dest * ROWS : dest * ROWS + OWN] = z_rows[dest * OWN : (dest + 1) * OWN].astype(BF16)
    moves[4].wait()
    tap_rows = t_buf[...].astype(F32)
    for dest in range(spans):
        base = dest * ROWS
        group = dest * OWN // GROUP
        tail = jnp.broadcast_to(tap_rows[group : group + 1], (2, tap_rows.shape[1]))
        packed[base + 2 * OWN : base + ROWS] = tail.astype(BF16)
    moves[2].wait()
    moves[3].wait()
    g_rows = product(o_buf[...], q_buf[...]).T.astype(F32)
    for dest in range(spans):
        here = slice(dest * OWN, (dest + 1) * OWN)
        base = dest * ROWS
        packed[base + OWN : base + 2 * OWN] = g_rows[here].astype(BF16)
    moves[5].wait()
    moves[6].wait()


def conv_body(scale, reaches, gain, packed, out, shifted, acc_ref):
    spans, block_len = packed.shape[0] // ROWS, packed.shape[1]
    wide = 2 * block_len
    half = spans // 2
    owner = lax.axis_index("ctx")
    place = lax.broadcasted_iota(jnp.int32, (1, reaches.shape[1]), 1)
    reach = jnp.sum(jnp.where(place == owner * 8 // GROUP, reaches[...].astype(F32), 0.0), axis=1, keepdims=True)
    place = lax.broadcasted_iota(jnp.int32, (8, gain.shape[1]), 1)
    channel = lax.broadcasted_iota(jnp.int32, (8, gain.shape[1]), 0) + owner * 8
    own_gain = jnp.sum(jnp.where(place == channel, gain[...], 0.0), axis=1, keepdims=True)
    row = lax.broadcasted_iota(jnp.int32, (block_len, block_len), 0)
    col = lax.broadcasted_iota(jnp.int32, (block_len, block_len), 1)
    upper = col >= row
    flip = eye(block_len, True)

    tiles = [packed[span * ROWS : span * ROWS + 2 * OWN].astype(F32) for span in range(spans)]
    z_list = [tile[:OWN] for tile in tiles]
    g_list = [tile[OWN:] for tile in tiles]
    taps = [packed[(span + 1) * ROWS - 2 : (span + 1) * ROWS].astype(F32)[:1] for span in range(spans)]
    reach = jnp.broadcast_to(reach, (8, block_len))
    weights = [
        jnp.concatenate([jnp.where(reach > offset, 1.0, 0.0)] * (block_len // 8), axis=0)
        for offset in range(spans)
    ]

    g_all = jnp.concatenate(g_list, axis=0).astype(BF16)
    g_flip = matmul(g_all, flip)
    z_flip = matmul(jnp.concatenate(z_list, axis=0).astype(BF16), flip)
    z_down = jnp.concatenate([jnp.zeros((8, block_len), F32), z_flip[:-8]], axis=0)
    shifted[0 : spans * 8] = jnp.zeros((spans * 8, wide), BF16)
    shifted[spans * 8 : spans * 16] = jnp.concatenate([z_flip, z_down], axis=1).astype(BF16)
    g_turn = jnp.concatenate(g_list, axis=0).T.astype(BF16)
    parts = []
    for pair in range(half):
        first = 2 * pair
        parts.append(jnp.concatenate([z_list[first], z_list[first + 1]], axis=1))
        low, high = (spans - 1 - first) * 8, (spans - 2 - first) * 8
        parts.append(jnp.concatenate([g_flip[low : low + 8], g_flip[high : high + 8]], axis=1))
    data = jnp.concatenate(parts, axis=0).astype(BF16)

    before = jnp.zeros((block_len, block_len), F32)
    odd = jnp.zeros((block_len, block_len), BF16)
    acc = None
    sum_rows = []
    last = None
    for pair in range(half):
        blocks = [odd]
        for offset in (2 * pair, 2 * pair + 1):
            window = jnp.broadcast_to(taps[offset], (block_len, block_len))
            turned = pltpu.roll(window, 0, 1, stride=1, stride_axis=0)
            block = jnp.where(col >= row, turned, before).astype(BF16)
            blocks.append(block * weights[offset].astype(BF16))
            before = turned
        odd = blocks[2]
        block = jnp.concatenate(
            [jnp.concatenate(blocks[1:], axis=1), jnp.concatenate(blocks[:2], axis=1)], axis=0
        )
        term = matmul(data[: (half - pair) * 16], block)
        if acc is None:
            acc = acc_ref
            acc[...] = term
        else:
            acc[pair * 16 :] += term
        start = spans * 8 - 16 * pair
        prods = matmul(g_turn, shifted[start : start + spans * 8])
        for side in range(2):
            own = prods[:, side * block_len : (side + 1) * block_len] * weights[2 * pair + side]
            own = pltpu.roll(own, 1, 1, stride=1, stride_axis=0)
            if last is not None:
                sum_rows.append(jnp.sum(jnp.where(col <= row, last, own), axis=0, keepdims=True))
            last = own
    sum_rows.append(jnp.sum(jnp.where(col <= row, last, 0.0), axis=0, keepdims=True))

    skip = jnp.zeros((8, block_len), F32)
    for span in range(spans):
        skip = skip + z_list[span] * g_list[span]
    skip = jnp.sum(skip, axis=1, keepdims=True)
    lane = lax.broadcasted_iota(jnp.int32, (8, block_len), 1)
    sub = lax.broadcasted_iota(jnp.int32, (8, block_len), 0)
    skip_row = jnp.sum(jnp.where(lane % 8 == sub, skip, 0.0), axis=0, keepdims=True)
    high = skip_row.astype(BF16).astype(F32)
    skip_row = jnp.where(lane[:1] < block_len // 2, high, skip_row - high)

    for span in range(spans):
        pair, side = span // 2, span % 2
        forth = acc[pair * 16 : pair * 16 + 8, side * block_len : (side + 1) * block_len]
        mirror = spans - 1 - span
        pair, side = mirror // 2, mirror % 2
        back = acc[pair * 16 + 8 : pair * 16 + 16, side * block_len : (side + 1) * block_len]
        sums = sum_rows[span]
        forth = forth * scale + own_gain * z_list[span]
        back = back * scale + own_gain * g_flip[span * 8 : span * 8 + 8]
        base = span * ROWS
        out[base : base + 2 * OWN] = jnp.concatenate([forth, back], axis=0).astype(BF16)
        out[base + 2 * OWN : base + ROWS] = jnp.concatenate([sums, skip_row], axis=0).astype(BF16)


def gate_body(scale, query, key, value, cotangent, packed, mixed, query_grad, key_grad, value_grad, tap_grad, skip_grad, q_buf, o_buf, k_buf, v_buf, t_buf, s_buf, sems):
    spans, block_len = packed.shape[0] // ROWS, packed.shape[1]
    moves = []

    def send(source, target):
        moves.append(pltpu.make_async_copy(source, target, sems.at[len(moves)]))
        moves[-1].start()

    tiles = [packed[span * ROWS : span * ROWS + 2 * OWN].astype(F32) for span in range(spans)]
    tails = [packed[(span + 1) * ROWS - 2 : (span + 1) * ROWS].astype(F32) for span in range(spans)]
    total = jnp.concatenate([tile[:OWN] for tile in tiles], axis=0).T
    q_buf[...] = (query[...].astype(F32) * total).astype(BF16)
    send(q_buf, mixed)
    o_buf[...] = (cotangent[...].astype(F32) * total).astype(BF16)
    send(o_buf, query_grad)
    back = jnp.concatenate([tile[OWN:] for tile in tiles], axis=0).astype(BF16)
    total = matmul_nt(eye(block_len, True), back)
    k_buf[...] = (value[...].astype(F32) * total).astype(BF16)
    send(k_buf, key_grad)
    v_buf[...] = (key[...].astype(F32) * total).astype(BF16)
    send(v_buf, value_grad)

    per_group = GROUP // 8
    for group in range(spans // per_group):
        line = jnp.zeros((1, block_len), F32)
        for member in range(per_group):
            line = line + tails[group * per_group + member][0:1]
        t_buf[group : group + 1] = line * scale
    send(t_buf, tap_grad)

    lane = lax.broadcasted_iota(jnp.int32, (1, block_len), 1)
    per_row = block_len // OWN
    for part in range(s_buf.shape[1] // block_len):
        line = jnp.zeros((1, block_len), F32)
        other = jnp.zeros((1, block_len), F32)
        for place in range(per_row):
            piece = tails[part * per_row + place][1:2]
            line = jnp.where(lane // OWN == place, piece, line)
            other = jnp.where(lane // OWN == (place + per_row // 2) % per_row, piece, other)
        line = line + pltpu.roll(other, block_len // 2, 1)
        s_buf[:, part * block_len : (part + 1) * block_len] = line
    send(s_buf, skip_grad)
    for move in moves:
        move.wait()


def whole(space=pltpu.VMEM):
    return pl.BlockSpec(memory_space=space)


PARAMS = pltpu.CompilerParams(vmem_limit_bytes=48 * 1024 * 1024)


def pack(query_seq, key_seq, value_seq, out_grad, taps, gain, reaches, spans):
    block_len, width = query_seq.shape
    sources = [query_seq, key_seq, value_seq, out_grad, taps, gain, reaches]
    return pl.pallas_call(
        pack_body,
        out_shape=(
            jax.ShapeDtypeStruct((spans * ROWS, block_len), BF16),
            jax.ShapeDtypeStruct(gain.shape, gain.dtype),
            jax.ShapeDtypeStruct(reaches.shape, reaches.dtype),
        )
        + (jax.ShapeDtypeStruct((block_len, width), BF16),) * 4,
        in_specs=[whole(pltpu.HBM)] * 7,
        out_specs=[whole()] * 7,
        scratch_shapes=[pltpu.VMEM(taps.shape, BF16), pltpu.SemaphoreType.DMA((7,))],
        compiler_params=PARAMS,
        name="pack",
    )(*[pltpu.with_memory_space_constraint(x, pltpu.HBM) for x in sources])


def conv(reaches, gain, packed, scale):
    spans, block_len = packed.shape[0] // ROWS, packed.shape[1]
    return pl.pallas_call(
        functools.partial(conv_body, scale),
        out_shape=jax.ShapeDtypeStruct(packed.shape, BF16),
        in_specs=[whole()] * 3,
        out_specs=whole(),
        scratch_shapes=[
            pltpu.VMEM((spans * 16, 2 * block_len), BF16),
            pltpu.VMEM((spans * 8, 2 * block_len), F32),
        ],
        compiler_params=PARAMS,
        name="conv",
    )(reaches, gain, packed)


def gate(query_seq, key_seq, value_seq, out_grad, packed, scale):
    block_len, width = query_seq.shape
    act = jax.ShapeDtypeStruct((block_len, width), BF16)
    act_buf = pltpu.VMEM((block_len, width), BF16)
    tap_shape, skip_shape = (width // GROUP, block_len), (1, width)
    return pl.pallas_call(
        functools.partial(gate_body, scale),
        out_shape=(act,) * 4
        + (jax.ShapeDtypeStruct(tap_shape, F32), jax.ShapeDtypeStruct(skip_shape, F32)),
        in_specs=[whole()] * 5,
        out_specs=[whole(pltpu.HBM)] * 6,
        scratch_shapes=[act_buf] * 4
        + [pltpu.VMEM(tap_shape, F32), pltpu.VMEM(skip_shape, F32), pltpu.SemaphoreType.DMA((6,))],
        compiler_params=PARAMS,
        name="gate",
    )(query_seq, key_seq, value_seq, out_grad, packed)


def exchange(packed, spans):
    paired = packed.reshape(spans, ROWS // 2, 2, packed.shape[1])
    return lax.all_to_all(paired, "ctx", 0, 0, tiled=True).reshape(packed.shape)


def body(query_seq, key_seq, value_seq, out_grad, filters, skip_gain, reaches):
    spans = lax.axis_size("ctx")
    scale = 1.0 / math.sqrt(query_seq.shape[0] * spans)
    acts = (query_seq, key_seq, value_seq, out_grad)
    packed, gain, reaches, *acts = pack(*acts, filters.T, skip_gain[None, :], reaches[None, :], spans)
    packed = exchange(packed, spans)
    packed = conv(reaches, gain, packed, scale)
    packed = exchange(packed, spans)
    *grads, tap_grad, skip_grad = gate(*acts, packed, scale)
    return (*grads, tap_grad.T, skip_grad[0])


def solution(mesh):
    spec = P("ctx", "ch")
    return jax.shard_map(
        body,
        mesh=mesh,
        in_specs=(spec, spec, spec, spec, spec, P("ch"), P("ch")),
        out_specs=(spec, spec, spec, spec, spec, P("ch")),
        check_vma=False,
    )
```
